32 devices in a mesh: dp: 4 (over z), gx: 4 (over y, core), gy: 2 (over x).
Axes of the slice: x: 2, y: 2, z: 4, core: 2. Of those that a mesh axis runs over, the one named last changes fastest.
Arguments:
- features: bfloat16 [64, 96, 512], P(('dp', 'gx', 'gy')), parts along dimension 0, may hold values from -6 to 6
- occupancy: int32 [64, 18], P(('dp', 'gx', 'gy')), parts along dimension 0, may hold values from 0 to 1073741823, as said below
- neighbours: int32 [64, 27], P(('dp', 'gx', 'gy')), parts along dimension 0, may hold values from -1 to 33, as said below
- send_slots: int32 [32, 4, 2], P(('dp', 'gx'), 'gy'), parts along dimension 0, may hold values from -1 to 1, as said below
- weight_a: bfloat16 [27, 96, 96], replicated, may hold values from -0.125 to 0.125
- weight_b: bfloat16 [27, 96, 256], replicated, may hold values from -0.125 to 0.125
- cotangent: bfloat16 [64, 256, 512], P(('dp', 'gx', 'gy')), parts along dimension 0, may hold values from -6 to 6
Outputs:
- layer_out: bfloat16 [64, 256, 512], P(('dp', 'gx', 'gy')), parts along dimension 0
- grad_features: bfloat16 [64, 96, 512], P(('dp', 'gx', 'gy')), parts along dimension 0
- grad_weight_a: float32 [108, 96, 96], P('dp'), parts along dimension 0
- grad_weight_b: float32 [108, 96, 256], P('dp'), parts along dimension 0
The draws below stay inside these ranges and needn't reach their ends.
There are 4 independent parts, one for each index of `dp`. The reference program is written for one: setup_inputs(seed, part) draws one part's arguments, and reference() takes and returns one part's arrays. A program takes and returns all parts, laid end to end along the dimension named above; an argument that names none is the same for every part. Nothing has to cross between parts.
Inputs may be any that keep to these rules, and one draw needn't show every extreme that they name: Tile (i, j) covers brick positions X in 2 i, 2 i + 1 and Y in 2 j, 2 j + 1 with all Z; its bricks fill its slots from 0 upward in the order of (X, Y, Z), and send_slots names each of them at its position; every tile holds 1 to 2 bricks, and some tile holds 2. `neighbours`: for a slot holding a brick, entry 9 (a+1) + 3 (b+1) + (c+1) is the table index of the brick at brick offset (a, b, c): its slot if that brick lies in the same tile, the index of its cell in the table if it lies in a neighbouring tile, -1 if no brick is there; entry 13 is the slot itself; slots without a brick hold -1 throughout. `occupancy`: slots without a brick are all zero.
All inputs are finite; a program needn't handle non-finite values.
Results may differ from the reference program's by a relative error of at most 0.0051.
Values may be sent and summed in bfloat16 or wider, within the bound.
No kernel may reach another device: no remote copies, remote signals or barrier semaphores. Data moves between devices by JAX's collectives and lax.ppermute only.
A program may use at most 128 MiB of HBM per device.

```python
import jax
import jax.numpy as jnp
from jax import lax

EDGE = 8
VOX = 512
TAPS = 27
WORDS = 18
CH_MID = 96
CH_OUT = 256
LAYERS = 2
SLOTS = 2
TILES_X = 4
TILES_Y = 2
BRICKS = 16


def brick_layout(key):
    tile_count = TILES_X * TILES_Y
    places = 4 * LAYERS
    key_count, key_top, key_order = jax.random.split(key, 3)
    counts = jax.random.randint(key_count, (tile_count,), 1, SLOTS + 1)
    fullest = jax.random.randint(key_top, (), 0, tile_count)
    counts = jnp.where(jnp.arange(tile_count) == fullest, SLOTS, counts)
    rank_of = jax.vmap(lambda sub_key: jax.random.permutation(sub_key, places))(jax.random.split(key_order, tile_count))
    occupied = rank_of < counts[:, None]
    slot_ids = jnp.where(occupied, jnp.cumsum(occupied.astype(jnp.int32), axis=1) - 1, -1)
    grid_slots = slot_ids.reshape(TILES_X, TILES_Y, 2, 2, LAYERS).transpose(0, 2, 1, 3, 4).reshape(2 * TILES_X, 2 * TILES_Y, LAYERS)
    return (counts, slot_ids, grid_slots)


def draw_send_slots(key, part):
    return brick_layout(jax.random.fold_in(key, 11))[2].astype(jnp.int32)


def draw_neighbours(key, part):
    counts, slot_ids, grid_slots = brick_layout(jax.random.fold_in(key, 11))
    tile_count = TILES_X * TILES_Y
    places = 4 * LAYERS
    matched = slot_ids[:, :, None] == jnp.arange(SLOTS)[None, None, :]
    position = jnp.sum(jnp.where(matched, jnp.arange(places)[None, :, None], 0), axis=1)
    used_slot = jnp.arange(SLOTS)[None, :] < counts[:, None]
    tile_x = (jnp.arange(tile_count) // TILES_Y)[:, None]
    tile_y = (jnp.arange(tile_count) % TILES_Y)[:, None]
    base_x = 2 * tile_x + position // (2 * LAYERS)
    base_y = 2 * tile_y + position // LAYERS % 2
    base_z = position % LAYERS
    offsets = jnp.arange(27)
    step_x = offsets // 9 - 1
    step_y = offsets // 3 % 3 - 1
    step_z = offsets % 3 - 1
    reach_x = base_x[:, :, None] + step_x[None, None, :]
    reach_y = base_y[:, :, None] + step_y[None, None, :]
    reach_z = base_z[:, :, None] + step_z[None, None, :]
    inside = (reach_x >= 0) & (reach_x < 2 * TILES_X) & (reach_y >= 0) & (reach_y < 2 * TILES_Y) & (reach_z >= 0) & (reach_z < LAYERS)
    found = grid_slots[jnp.clip(reach_x, 0, 2 * TILES_X - 1), jnp.clip(reach_y, 0, 2 * TILES_Y - 1), jnp.clip(reach_z, 0, LAYERS - 1)]
    same_tile = (reach_x // 2 == tile_x[:, :, None]) & (reach_y // 2 == tile_y[:, :, None])
    border_id = SLOTS + ((reach_x - 2 * tile_x[:, :, None] + 1) * 4 + (reach_y - 2 * tile_y[:, :, None] + 1)) * LAYERS + reach_z
    linked = jnp.where(same_tile, found, border_id)
    linked = jnp.where(inside & (found >= 0) & used_slot[:, :, None], linked, -1)
    return linked.reshape(tile_count * SLOTS, 27).astype(jnp.int32)


def draw_occupancy(key, part):
    counts, slot_ids, grid_slots = brick_layout(jax.random.fold_in(key, 11))
    tile_count = TILES_X * TILES_Y
    packed_bits = jax.random.randint(jax.random.fold_in(key, 12), (tile_count, SLOTS, WORDS), 0, 2 ** 30)
    used_slot = jnp.arange(SLOTS)[None, :] < counts[:, None]
    return jnp.where(used_slot[:, :, None], packed_bits, 0).reshape(tile_count * SLOTS, WORDS).astype(jnp.int32)


def block_levels(rng, shape, shards, low, top_value):
    loudness = 1.0
    for axis_at, shards_of in shards:
        draws = jax.random.uniform(jax.random.fold_in(jax.random.fold_in(rng, 6), axis_at), (shards_of,), jnp.float32, low / len(shards), top_value / len(shards))
        loudness = loudness * jnp.repeat(jnp.exp(draws), shape[axis_at] // shards_of).reshape((-1,) + (1,) * (len(shape) - 1 - axis_at))
    return loudness


def scatter_about(key, extent, deviation, reach, cuts=(), kind=jnp.bfloat16):
    drawn = deviation * jax.random.normal(key, extent, jnp.float32)
    if cuts:
        drawn = drawn * block_levels(key, extent, cuts, -0.22, 0.18)
    return jnp.clip(drawn, -reach, reach).astype(kind)


def setup_inputs(seed: int = 0, part: int = 0) -> dict:
    seeds = jax.random.split(jax.random.key(seed), 8)
    own_keys = jax.random.split(jax.random.fold_in(seeds[7], part), 8)
    return {
        "features": scatter_about(own_keys[0], (BRICKS, CH_MID, VOX), 1.0, 6.0, ((0, 8),)),
        "occupancy": draw_occupancy(jax.random.fold_in(jax.random.fold_in(seeds[7], part), 71), part),
        "neighbours": draw_neighbours(jax.random.fold_in(jax.random.fold_in(seeds[7], part), 71), part),
        "send_slots": draw_send_slots(jax.random.fold_in(jax.random.fold_in(seeds[7], part), 71), part),
        "weight_a": scatter_about(seeds[4], (TAPS, CH_MID, CH_MID), (TAPS * CH_MID) ** -0.5, 0.125),
        "weight_b": scatter_about(seeds[5], (TAPS, CH_MID, CH_OUT), (TAPS * CH_MID) ** -0.5, 0.125),
        "cotangent": scatter_about(own_keys[6], (BRICKS, CH_OUT, VOX), 1.0, 6.0, ((0, 8),)),
    }


def unpack_mask(occupancy):
    shifts = jnp.arange(30, dtype=jnp.int32)
    bit_flags = jnp.right_shift(occupancy[:, :, None], shifts[None, None, :]) & 1
    return bit_flags.reshape(occupancy.shape[0], -1)[:, :VOX].astype(jnp.float32)

def assemble(slot_table, neighbours):
    bottom = slot_table.shape[0] - 1
    pointer = jnp.where(neighbours < 0, bottom, neighbours).astype(jnp.int32)
    ranges = (slice(EDGE - 1, EDGE), slice(0, EDGE), slice(0, 1))
    planes = []
    for along_x in range(3):
        columns = []
        for along_y in range(3):
            pieces = []
            for along_z in range(3):
                chosen = jnp.take(slot_table, pointer[:, 9 * along_x + 3 * along_y + along_z], axis=0)
                chosen = chosen.reshape(chosen.shape[0], chosen.shape[1], EDGE, EDGE, EDGE)
                pieces.append(chosen[:, :, ranges[along_x], ranges[along_y], ranges[along_z]])
            columns.append(jnp.concatenate(pieces, axis=4))
        planes.append(jnp.concatenate(columns, axis=3))
    return jnp.concatenate(planes, axis=2)

def unfold(padded):
    brick_count = padded.shape[0]
    channels = padded.shape[1]
    windows = []
    for tap_x in range(3):
        for tap_y in range(3):
            for tap_z in range(3):
                windows.append(padded[:, :, tap_x:tap_x + EDGE, tap_y:tap_y + EDGE, tap_z:tap_z + EDGE].reshape(brick_count, channels, VOX))
    return jnp.stack(windows, axis=1)

def build_tables(bricks_in, send_slots):
    tile_count = TILES_X * TILES_Y
    channels = bricks_in.shape[1]
    grid_x = jnp.arange(2 * TILES_X, dtype=jnp.int32)[:, None, None]
    grid_y = jnp.arange(2 * TILES_Y, dtype=jnp.int32)[None, :, None]
    owner = grid_x // 2 * TILES_Y + grid_y // 2
    rows_all = jnp.where(send_slots < 0, BRICKS, owner * SLOTS + send_slots).astype(jnp.int32)
    extended = jnp.concatenate([bricks_in, jnp.zeros((1, channels, VOX), bricks_in.dtype)], axis=0)
    grid_cells = jnp.take(extended, rows_all.reshape(-1), axis=0).reshape(2 * TILES_X, 2 * TILES_Y, LAYERS, channels, VOX)
    padded = jnp.pad(grid_cells, ((1, 1), (1, 1), (0, 0), (0, 0), (0, 0)))
    border_cells = []
    for row_off in range(4):
        for col_off in range(4):
            border_cells.append(padded[row_off:row_off + 2 * TILES_X:2, col_off:col_off + 2 * TILES_Y:2])
    border = jnp.stack(border_cells, axis=2).reshape(tile_count, 16 * LAYERS, channels, VOX)
    own_rows = bricks_in.reshape(tile_count, SLOTS, channels, VOX)
    blank_rows = jnp.zeros((tile_count, 1, channels, VOX), bricks_in.dtype)
    return jnp.concatenate([own_rows, border, blank_rows], axis=1)

def conv_forward(slot_table, neighbours, weight, voxel_mask):
    patches = unfold(assemble(slot_table, neighbours)).astype(jnp.float32)
    summed = jnp.einsum('nkcv,kcd->ndv', patches, weight.astype(jnp.float32), precision=lax.Precision.HIGHEST)
    return summed * voxel_mask[:, None, :]

def conv_backward(slot_table, neighbours, weight, grad_out):
    patches = unfold(assemble(slot_table, neighbours)).astype(jnp.float32)
    grad_wide = grad_out.astype(jnp.float32)
    grad_weight = jnp.einsum('nkcv,ndv->kcd', patches, grad_wide, precision=lax.Precision.HIGHEST)
    grad_patches = jnp.einsum('kcd,ndv->nkcv', weight.astype(jnp.float32), grad_wide, precision=lax.Precision.HIGHEST)
    primal = jnp.zeros(slot_table.shape, jnp.float32)
    unused, pullback = jax.vjp(lambda values: unfold(assemble(values, neighbours)), primal)
    return (grad_weight, pullback(grad_patches)[0])

def reference(features, occupancy, neighbours, send_slots, weight_a, weight_b, cotangent):
    tile_count = TILES_X * TILES_Y
    voxel_mask = unpack_mask(occupancy)
    mask_wide = voxel_mask[:, None, :]
    inputs = (features.astype(jnp.float32) * mask_wide).astype(jnp.bfloat16)
    tile_links = neighbours.reshape(tile_count, SLOTS, TAPS)
    mask_tiles = voxel_mask.reshape(tile_count, SLOTS, VOX)

    def run_forward(bricks_in, weight):
        tables = build_tables(bricks_in, send_slots)
        outcome = lax.map(lambda packed: conv_forward(packed[0], packed[1], weight, packed[2]), (tables, tile_links, mask_tiles))
        return (tables, outcome.reshape(BRICKS, weight.shape[2], VOX))

    def run_backward(tables, bricks_shape, weight, gradient):
        grad_tiles = gradient.reshape(tile_count, SLOTS, gradient.shape[1], VOX)

        def scan_step(running, packed):
            grad_weight, grad_table = conv_backward(packed[0], packed[1], weight, packed[2])
            return (running + grad_weight, grad_table)
        initial = jnp.zeros(weight.shape, jnp.float32)
        summed_w, grad_tables = lax.scan(scan_step, initial, (tables, tile_links, grad_tiles))
        primal = jnp.zeros(bricks_shape, jnp.float32)
        unused, pullback = jax.vjp(lambda values: build_tables(values, send_slots), primal)
        return (summed_w, pullback(grad_tables)[0])
    tables_x, pre_a = run_forward(inputs, weight_a)
    hidden = jax.nn.silu(pre_a).astype(jnp.bfloat16)
    tables_h, pre_b = run_forward(hidden, weight_b)
    layer_out = pre_b.astype(jnp.bfloat16)
    grad_out = (cotangent.astype(jnp.float32) * mask_wide).astype(jnp.bfloat16)
    grad_wb_sum, grad_hidden = run_backward(tables_h, hidden.shape, weight_b, grad_out)
    logistic = jax.nn.sigmoid(pre_a)
    grad_pre = (grad_hidden * logistic * (1.0 + pre_a * (1.0 - logistic)) * mask_wide).astype(jnp.bfloat16)
    grad_wa_sum, grad_inputs = run_backward(tables_x, inputs.shape, weight_a, grad_pre)
    grad_features = (grad_inputs * mask_wide).astype(jnp.bfloat16)
    norm_scale = float(BRICKS * VOX) ** (-0.5)
    return (layer_out, grad_features, grad_wa_sum * norm_scale, grad_wb_sum * norm_scale)
```

```python
import functools

import jax
import jax.numpy as jnp
from jax import lax
from jax.experimental import pallas as pl
from jax.experimental.pallas import tpu as pltpu
from jax.sharding import PartitionSpec as P

EDGE = 8
VOX = 512
TAPS = 27
PLANE = 80
PADDED = 896
OUTER = 640
FIRST = 88
FACE = 128
FAR = 100
BF = jnp.bfloat16
F32 = jnp.float32
VMEM = pl.BlockSpec(memory_space=pltpu.VMEM)
SMEM = pl.BlockSpec(memory_space=pltpu.SMEM)
LIMIT = 58 * 1024 * 1024


def iota(shape, dim):
    return lax.broadcasted_iota(jnp.int32, shape, dim)


def one_hot(cond):
    return jnp.where(cond, 1.0, 0.0).astype(BF)


def slot_places(send_ref):
    places = []
    for slot in range(2):
        px = py = pz = held = jnp.int32(0)
        for x in range(2):
            for y in range(2):
                for z in range(2):
                    here = (send_ref[x, y, z] == slot).astype(jnp.int32)
                    held = held + here
                    px = px + here * x
                    py = py + here * y
                    pz = pz + here * z
        places.append((px, py, pz, held))
    return places


def lane_mask(occ_ref, slot, width, plane, shift):
    lane = iota((8, width), 1)
    if plane == 64:
        voxel = lane
        inside = lane >= 0
    else:
        x = lax.shift_right_logical(lane * 205, 14)
        rest = lane - x * plane
        voxel = x * 64 + rest
        inside = rest < 64
    word = lax.shift_right_logical(voxel * 2185, 16)
    bit = voxel - word * 30
    total = jnp.zeros((8, width), jnp.int32)
    for w in range(18):
        total = jnp.where(word == w, occ_ref[slot, w], total)
    on = lax.shift_right_logical(total, bit) & 1
    return jnp.where(inside, on, 0).astype(F32)[:1]


def pack_sends(bricks, send_ref, sign_ref, dirs, plus_ref, minus_ref, y_ref, out_rows):
    channels = bricks.shape[0]
    group = channels // 4
    places = slot_places(send_ref)
    lane = iota((VOX, FACE), 1)
    row = iota((VOX, FACE), 0)
    i = row >> 6
    j = (row >> 3) & 7
    l = row & 7

    def product(targets, match):
        acc = None
        for slot in range(2):
            part = jnp.dot(
                bricks[:, VOX * slot : VOX * slot + VOX],
                one_hot(targets[slot] == match),
                preferred_element_type=F32,
            )
            acc = part if acc is None else acc + part
        return acc

    for side, ref in ((1, plus_ref), (0, minus_ref)):
        faces = []
        ahead = jnp.int32(0)
        for px, py, pz, held in places:
            facing = (px == side).astype(jnp.int32) * held
            target = jnp.where(
                (i == 7 * side) & (facing == 1), ahead * 64 + j * 8 + l, -1
            )
            faces.append(target)
            ahead = ahead + facing
        ref[:channels, :] = product(faces, lane).astype(BF)
        for q in range(dirs):
            col = (sign_ref[q] + 1) >> 1
            edges = []
            for px, py, pz, held in places:
                facing = (px == side) & (py == col) & (held == 1)
                target = jnp.where(
                    (i == 7 * side) & (j == 7 * col) & facing,
                    16 * (1 - side) + pz * 8 + l,
                    -1,
                )
                edges.append(target)
            wide = product(edges, lane & 31)
            packed = jnp.zeros((group, FACE), F32)
            glane = iota((group, FACE), 1) >> 5
            for g in range(4):
                packed = jnp.where(glane == g, wide[group * g : group * g + group], packed)
            ref[channels + group * q : channels + group * q + group, :] = packed.astype(BF)
    for q in range(dirs):
        col = (sign_ref[q] + 1) >> 1
        faces = []
        ahead = jnp.int32(0)
        for px, py, pz, held in places:
            facing = (py == col).astype(jnp.int32) * held
            target = jnp.where(
                (j == 7 * col) & (facing == 1), ahead * 64 + i * 8 + l, -1
            )
            faces.append(target)
            ahead = ahead + facing
        y_ref[q, :, :] = product(faces, lane).astype(BF)


def encode(x, y, z, ok):
    ok = ok & (x >= 0) & (x <= 9) & (y >= 0) & (y <= 9) & (z >= -1) & (z <= 8)
    deep = jnp.where(z < 0, PADDED, jnp.where(z > 7, PADDED + 7, z))
    return jnp.where(ok, x * PLANE + y * 8 + deep, -1)


def fill_targets(t_ref, n, send_ref, near_ref, sign_ref, dirs):
    places = slot_places(send_ref)
    nx, ny, nz, held = places[n]
    row = iota((VOX, FACE), 0)
    for slot in range(2):
        px, py, pz, _ = places[slot]
        t_ref[VOX * slot : VOX * slot + VOX, :] = encode(
            (row >> 6) + 1 + 8 * (px - nx),
            ((row >> 3) & 7) + 1 + 8 * (py - ny),
            (row & 7) + 8 * (pz - nz),
            row >= 0,
        )

    def ranked(offset_of):
        count = jnp.int32(0)
        firsts = [jnp.int32(FAR), jnp.int32(FAR)]
        depths = [jnp.int32(0), jnp.int32(0)]
        for across in range(2):
            for z in range(2):
                there = (near_ref[n, offset_of(across, z)] >= 0).astype(jnp.int32)
                for rank in range(2):
                    take = (there == 1) & (count == rank)
                    firsts[rank] = jnp.where(take, across, firsts[rank])
                    depths[rank] = jnp.where(take, z, depths[rank])
                count = count + there
        return firsts, depths

    row = iota((FACE, FACE), 0)
    high = row >= 64
    u = (row >> 3) & 7
    l = row & 7
    firsts, depths = ranked(
        lambda across, z: 18 * nx + 3 * (across - ny + 1) + (z - nz + 1)
    )
    across = jnp.where(high, firsts[1], firsts[0])
    depth = jnp.where(high, depths[1], depths[0])
    for side in range(2):
        t_ref[1024 + FACE * side : 1024 + FACE * side + FACE, :] = encode(
            jnp.full((FACE, FACE), 9 * side, jnp.int32),
            u + 1 + 8 * (across - ny),
            l + 8 * (depth - nz),
            jnp.broadcast_to(nx == side, (FACE, FACE)),
        )
    firsts, depths = ranked(
        lambda across, z: 9 * (across - nx + 1) + 6 * ny + (z - nz + 1)
    )
    across = jnp.where(high, firsts[1], firsts[0])
    depth = jnp.where(high, depths[1], depths[0])
    for q in range(dirs):
        side = (sign_ref[dirs + q] + 1) >> 1
        at = 1280 + FACE * q
        t_ref[at : at + FACE, :] = encode(
            u + 1 + 8 * (across - nx),
            jnp.zeros((FACE, FACE), jnp.int32) + 9 * side,
            l + 8 * (depth - nz),
            jnp.broadcast_to(ny == side, (FACE, FACE)),
        )
        at = 1280 + FACE * dirs + FACE * q
        e = row & 31
        from_side = e >> 4
        t_ref[at : at + FACE, :] = encode(
            9 * from_side,
            jnp.zeros((FACE, FACE), jnp.int32) + 9 * side,
            (e & 7) + 8 * (((e >> 3) & 1) - nz),
            (from_side == nx) & (ny == side),
        )


def gather_sources(d_ref, own, recv_minus, recv_plus, recv_y, dirs):
    channels = own.shape[0]
    group = channels // 4
    d_ref[:, :1024] = own
    d_ref[:, 1024:1152] = recv_minus[:channels, :]
    d_ref[:, 1152:1280] = recv_plus[:channels, :]
    glane = iota((group, FACE), 1) >> 5
    for q in range(dirs):
        at = 1280 + FACE * q
        d_ref[:, at : at + FACE] = recv_y[q, :channels, :]
        packed = recv_y[q, channels : channels + group, :].astype(F32)
        spread = jnp.concatenate(
            [jnp.where(glane == g, packed, 0.0) for g in range(4)], axis=0
        )
        at = 1280 + FACE * dirs + FACE * q
        d_ref[:, at : at + FACE] = spread.astype(BF)


def fill_padded(d_ref, t_ref, sel_ref, z_refs, send_ref, near_ref, sign_ref, dirs):
    sources = d_ref.shape[1]
    for n in range(2):
        fill_targets(t_ref, n, send_ref, near_ref, sign_ref, dirs)
        parts = []
        for half in range(2):
            for b in range(7):
                sel_ref[:, 128 * b : 128 * b + 128] = one_hot(
                    t_ref[...] == iota((sources, 128), 1) + (PADDED * half + 128 * b)
                )
            if half == 0:
                out = jnp.dot(d_ref[...], sel_ref[...], preferred_element_type=F32)
            else:
                other = VOX * (1 - n)
                out = jnp.dot(
                    d_ref[:, other : other + VOX],
                    sel_ref[other : other + VOX, :],
                    preferred_element_type=F32,
                ) + jnp.dot(
                    d_ref[:, 1024:], sel_ref[1024:, :], preferred_element_type=F32
                )
            parts.append(out)
        middle, ends = parts
        for ref, start, rows in z_refs:
            mid = middle[start : start + rows]
            end = ends[start : start + rows]
            l = iota((rows, PADDED), 1) & 7
            at = slice(PADDED * n, PADDED * n + PADDED)
            ref[1, :, at] = mid.astype(BF)
            ref[0, :, at] = jnp.where(l == 0, end, pltpu.roll(mid, 1, 1)).astype(BF)
            ref[2, :, at] = jnp.where(l == 7, end, pltpu.roll(mid, PADDED - 1, 1)).astype(BF)


def tap_lanes(k, n, flip):
    a, b, c = k // 9, k // 3 % 3, k % 3
    if flip:
        a, b, c = 2 - a, 2 - b, 2 - c
    at = PADDED * n + PLANE * a + 8 * b
    return c, slice(at, at + OUTER)


def fill_patches(p_ref, z_ref, flip):
    channels = z_ref.shape[1]
    for k in range(TAPS):
        for n in range(2):
            c, lanes = tap_lanes(k, n, flip)
            p_ref[channels * k : channels * k + channels, OUTER * n : OUTER * n + OUTER] = z_ref[
                c, :, lanes
            ]


def compaction():
    row = iota((OUTER, VOX), 0)
    x = lax.shift_right_logical(row * 205, 14)
    rest = row - x * PLANE
    return one_hot(jnp.where(rest < 64, x * 64 + rest, -1) == iota((OUTER, VOX), 1))


def mask_outer(occ_ref):
    return jnp.concatenate(
        [lane_mask(occ_ref, n, OUTER, PLANE, 0) for n in range(2)], axis=1
    )


def pack_kernel(dirs, feat_ref, cot_ref, occ_ref, send_ref, sign_ref, own_ref, plus_ref, minus_ref, y_ref):
    for n in range(2):
        mask = lane_mask(occ_ref, n, VOX, 64, 0)
        at = slice(VOX * n, VOX * n + VOX)
        own_ref[:96, at] = jnp.where(mask > 0.5, feat_ref[n].astype(F32), 0.0).astype(BF)
        own_ref[96:, at] = jnp.where(mask > 0.5, cot_ref[n].astype(F32), 0.0).astype(BF)
    pack_sends(own_ref[...], send_ref, sign_ref, dirs, plus_ref, minus_ref, y_ref, 352)


def first_kernel(
    dirs, own_ref, fm_ref, fp_ref, fy_ref, occ_ref, near_ref, send_ref, sign_ref, wat_ref, wb_ref,
    zx_ref, gpre_ref, gout_ref, hid_ref, plus_ref, minus_ref, y_ref,
    d_ref, t_ref, sel_ref, zg_ref, p_ref, acc_ref,
):
    gather_sources(d_ref, own_ref[...], fm_ref, fp_ref, fy_ref, dirs)
    fill_padded(
        d_ref, t_ref, sel_ref, ((zx_ref, 0, 96), (zg_ref, 96, 256)), send_ref, near_ref, sign_ref, dirs
    )
    mask = mask_outer(occ_ref)
    for n in range(2):
        c, lanes = tap_lanes(13, n, False)
        at = slice(OUTER * n, OUTER * n + OUTER)
        gout_ref[:, at] = jnp.where(mask[:, at] > 0.5, zg_ref[c, :, lanes].astype(F32), 0.0).astype(BF)
    fill_patches(p_ref, zx_ref, False)
    pre = jnp.dot(wat_ref[...], p_ref[...], preferred_element_type=F32)
    for k in range(TAPS):
        parts = []
        for n in range(2):
            c, lanes = tap_lanes(k, n, True)
            parts.append(
                jnp.dot(wb_ref[k], zg_ref[c, :, lanes], preferred_element_type=F32)
            )
        both = jnp.concatenate(parts, axis=1)
        if k == 0:
            acc_ref[...] = both
        else:
            acc_ref[...] += both
    pre = pre * mask
    gate = 1.0 / (1.0 + jnp.exp(-pre))
    hidden = (pre * gate).astype(BF)
    grad_pre = (acc_ref[...] * gate * (1.0 + pre * (1.0 - gate)) * mask).astype(BF)
    gpre_ref[...] = grad_pre
    squeeze = compaction()
    for n in range(2):
        at = slice(OUTER * n, OUTER * n + OUTER)
        to = slice(VOX * n, VOX * n + VOX)
        hid_ref[:96, to] = jnp.dot(hidden[:, at], squeeze, preferred_element_type=F32).astype(BF)
        hid_ref[96:, to] = jnp.dot(grad_pre[:, at], squeeze, preferred_element_type=F32).astype(BF)
    pack_sends(hid_ref[...], send_ref, sign_ref, dirs, plus_ref, minus_ref, y_ref, 192)


NT = (((1,), (1,)), ((), ()))


def weight_a_kernel(scale, zx_ref, gpre_ref, out_ref, p_ref):
    fill_patches(p_ref, zx_ref, False)
    out_ref[...] = scale * lax.dot_general(
        p_ref[...], gpre_ref[...], NT, preferred_element_type=F32
    )


def weight_b_kernel(
    scale, dirs, own_ref, fm_ref, fp_ref, fy_ref, near_ref, send_ref, sign_ref, gout_ref,
    out_ref, zh_ref, zp_ref, d_ref, t_ref, sel_ref, p_ref,
):
    gather_sources(d_ref, own_ref[...], fm_ref, fp_ref, fy_ref, dirs)
    fill_padded(
        d_ref, t_ref, sel_ref, ((zh_ref, 0, 96), (zp_ref, 96, 96)), send_ref, near_ref, sign_ref, dirs
    )
    fill_patches(p_ref, zh_ref, False)
    rows = TAPS * 96
    out_ref[:rows, :] = scale * lax.dot_general(
        p_ref[...], gout_ref[...], NT, preferred_element_type=F32
    )
    out_ref[rows:, :] = jnp.zeros((out_ref.shape[0] - rows, 256), F32)


def last_kernel(occ_ref, zh_ref, zp_ref, wbt_ref, wag_ref, out_ref, grad_ref, p_ref):
    mask = mask_outer(occ_ref)
    squeeze = compaction()
    fill_patches(p_ref, zh_ref, False)
    out = (jnp.dot(wbt_ref[...], p_ref[...], preferred_element_type=F32) * mask).astype(BF)
    for n in range(2):
        at = slice(OUTER * n, OUTER * n + OUTER)
        out_ref[n] = jnp.dot(out[:, at], squeeze, preferred_element_type=F32).astype(BF)
    fill_patches(p_ref, zp_ref, True)
    grad = (jnp.dot(wag_ref[...], p_ref[...], preferred_element_type=F32) * mask).astype(BF)
    for n in range(2):
        at = slice(OUTER * n, OUTER * n + OUTER)
        grad_ref[n] = jnp.dot(grad[:, at], squeeze, preferred_element_type=F32).astype(BF)


def call(kernel, outs, ins, scratch=(), flops=0, moved=0):
    specs = [SMEM if jnp.issubdtype(x.dtype, jnp.integer) else VMEM for x in ins]
    return pl.pallas_call(
        kernel,
        out_shape=[jax.ShapeDtypeStruct(s, d) for s, d in outs],
        in_specs=specs,
        out_specs=[VMEM] * len(outs),
        scratch_shapes=[pltpu.VMEM(s, d) for s, d in scratch],
        compiler_params=pltpu.CompilerParams(vmem_limit_bytes=LIMIT),
        cost_estimate=pl.CostEstimate(flops=flops, bytes_accessed=moved, transcendentals=0),
    )(*ins)


def exchange(channels, plus, minus, faces, count_x, count_y):
    up = [(k, k + 1) for k in range(count_x - 1)]
    down = [(k + 1, k) for k in range(count_x - 1)]
    from_minus = lax.ppermute(plus, "gx", up)
    from_plus = lax.ppermute(minus, "gx", down)
    group = channels // 4
    dirs = faces.shape[0]
    if dirs == 1:
        perms = [[(0, 1), (1, 0)]]
    else:
        perms = [
            [(k, k + 1) for k in range(count_y - 1)],
            [(k + 1, k) for k in range(count_y - 1)],
        ]
    arrived = []
    for q in range(dirs):
        at = channels + group * q
        edges = from_minus[at : at + group] + from_plus[at : at + group]
        arrived.append(
            lax.ppermute(jnp.concatenate([faces[q], edges], axis=0), "gy", perms[q])
        )
    return from_minus, from_plus, jnp.stack(arrived, axis=0)


def sum_region(value, count_x, count_y):
    if count_x != 4 or count_y != 2:
        return lax.psum(value, ("gx", "gy"))
    gx = lax.axis_index("gx")
    bits = {"c": gx & 1, "y": gx >> 1, "x": lax.axis_index("gy")}
    perms = {
        "c": ("gx", [(k, k ^ 1) for k in range(4)]),
        "y": ("gx", [(k, k ^ 2) for k in range(4)]),
        "x": ("gy", [(0, 1), (1, 0)]),
    }
    half = value.shape[1] // 2
    pieces = [(value[:, :half], "cyx"), (value[:, half:], "cxy")]
    parts = []
    for piece, order in pieces:
        for step in order:
            rows = piece.shape[0] // 2
            low, high = piece[:rows], piece[rows:]
            sent = jnp.where(bits[step] == 0, high, low).astype(BF)
            kept = jnp.where(bits[step] == 0, low, high)
            piece = kept + lax.ppermute(sent, *perms[step]).astype(F32)
        piece = piece.astype(BF)
        for step in order[::-1]:
            other = lax.ppermute(piece, *perms[step])
            first = bits[step] == 0
            piece = jnp.concatenate(
                [jnp.where(first, piece, other), jnp.where(first, other, piece)], axis=0
            )
        parts.append(piece.astype(F32))
    return jnp.concatenate(parts, axis=1)


def body(features, occupancy, neighbours, send_slots, weight_a, weight_b, cotangent):
    count_x = lax.axis_size("gx")
    count_y = lax.axis_size("gy")
    dirs = 1 if count_y == 2 else 2
    if dirs == 1:
        toward = 1 - 2 * lax.axis_index("gy")
        signs = jnp.stack([toward, toward]).astype(jnp.int32)
    else:
        signs = jnp.array([1, -1, -1, 1], jnp.int32)
    scale = float(features.shape[0] * VOX * count_x * count_y) ** -0.5
    sources = 1280 + 2 * FACE * dirs
    wat = weight_a.transpose(2, 0, 1).reshape(96, TAPS * 96)
    wag = weight_a.transpose(1, 0, 2).reshape(96, TAPS * 96)
    wbt = weight_b.transpose(2, 0, 1).reshape(256, TAPS * 96)

    rows = 352 + 88 * dirs
    own, plus, minus, faces = call(
        functools.partial(pack_kernel, dirs),
        [((352, 1024), BF), ((rows, FACE), BF), ((rows, FACE), BF), ((dirs, 352, FACE), BF)],
        [features, cotangent, occupancy, send_slots, signs],
        flops=352 * 1024 * 1024,
        moved=2 * 1024 * 1024,
    )
    from_minus, from_plus, from_y = exchange(352, plus, minus, faces, count_x, count_y)

    rows = 192 + 48 * dirs
    zx, gpre, gout, hid, plus, minus, faces = call(
        functools.partial(first_kernel, dirs),
        [
            ((3, 96, 2 * PADDED), BF),
            ((96, 2 * OUTER), BF),
            ((256, 2 * OUTER), BF),
            ((192, 1024), BF),
            ((rows, FACE), BF),
            ((rows, FACE), BF),
            ((dirs, 192, FACE), BF),
        ],
        [own, from_minus, from_plus, from_y, occupancy, neighbours, send_slots, signs, wat, weight_b],
        [
            ((352, sources), BF),
            ((sources, 128), jnp.int32),
            ((sources, PADDED), BF),
            ((3, 256, 2 * PADDED), BF),
            ((TAPS * 96, 2 * OUTER), BF),
            ((96, 2 * OUTER), F32),
        ],
        flops=5 * 10**9,
        moved=8 * 1024 * 1024,
    )
    from_minus, from_plus, from_y = exchange(192, plus, minus, faces, count_x, count_y)
    (grad_wa,) = call(
        functools.partial(weight_a_kernel, scale),
        [((TAPS * 96, 96), F32)],
        [zx, gpre],
        [((TAPS * 96, 2 * OUTER), BF)],
        flops=10**9,
        moved=2 * 1024 * 1024,
    )
    grad_wb, zh, zp = call(
        functools.partial(weight_b_kernel, scale, dirs),
        [((2688, 256), F32), ((3, 96, 2 * PADDED), BF), ((3, 96, 2 * PADDED), BF)],
        [hid, from_minus, from_plus, from_y, neighbours, send_slots, signs, gout],
        [
            ((192, sources), BF),
            ((sources, 128), jnp.int32),
            ((sources, PADDED), BF),
            ((TAPS * 96, 2 * OUTER), BF),
        ],
        flops=2 * 10**9,
        moved=4 * 1024 * 1024,
    )
    grad_wa = lax.psum(grad_wa, ("gx", "gy")).reshape(TAPS, 96, 96)
    layer_out, grad_features = call(
        last_kernel,
        [((2, 256, VOX), BF), ((2, 96, VOX), BF)],
        [occupancy, zh, zp, wbt, wag],
        [((TAPS * 96, 2 * OUTER), BF)],
        flops=3 * 10**9,
        moved=6 * 1024 * 1024,
    )
    grad_wb = sum_region(grad_wb, count_x, count_y)[: TAPS * 96].reshape(TAPS, 96, 256)
    return layer_out, grad_features, grad_wa, grad_wb


def solution(mesh):
    in_specs = (
        P(("dp", "gx", "gy"), None, None),
        P(("dp", "gx", "gy"), None),
        P(("dp", "gx", "gy"), None),
        P(("dp", "gx"), "gy", None),
        P(),
        P(),
        P(("dp", "gx", "gy"), None, None),
    )
    out_specs = (
        P(("dp", "gx", "gy"), None, None),
        P(("dp", "gx", "gy"), None, None),
        P("dp", None, None),
        P("dp", None, None),
    )
    return jax.shard_map(body, mesh=mesh, in_specs=in_specs, out_specs=out_specs, check_vma=False)
```

```python
import functools

import jax
import jax.numpy as jnp
from jax import lax
from jax.experimental import pallas as pl
from jax.experimental.pallas import tpu as pltpu
from jax.sharding import PartitionSpec as P

EDGE = 8
VOX = 512
TAPS = 27
PLANE = 80
PADDED = 896
OUTER = 640
FIRST = 88
FACE = 128
FAR = 100
HALO = 512
HALF = 4096
STORED = 2688
NT = (((1,), (1,)), ((), ()))
BF = jnp.bfloat16
F32 = jnp.float32
VMEM = pl.BlockSpec(memory_space=pltpu.VMEM)
FAR_SPEC = pl.BlockSpec(memory_space=pltpu.HBM)
SMEM = pl.BlockSpec(memory_space=pltpu.SMEM)
LIMIT = 58 * 1024 * 1024
MIB = 1024 * 1024


def iota(shape, dim):
    return lax.broadcasted_iota(jnp.int32, shape, dim)


def one_hot(cond):
    return jnp.where(cond, 1.0, 0.0).astype(BF)


def slot_places(send_ref):
    places = []
    for slot in range(2):
        px = py = pz = held = jnp.int32(0)
        for x in range(2):
            for y in range(2):
                for z in range(2):
                    here = (send_ref[x, y, z] == slot).astype(jnp.int32)
                    held = held + here
                    px = px + here * x
                    py = py + here * y
                    pz = pz + here * z
        places.append((px, py, pz, held))
    return places


def lane_mask(occ_ref, slot, width, plane):
    lane = iota((8, width), 1)
    if plane == 64:
        voxel = lane
        inside = lane >= 0
    else:
        x = lax.shift_right_logical(lane * 205, 14)
        rest = lane - x * plane
        voxel = x * 64 + rest
        inside = rest < 64
    word = lax.shift_right_logical(voxel * 2185, 16)
    bit = voxel - word * 30
    total = jnp.zeros((8, width), jnp.int32)
    for w in range(18):
        total = jnp.where(word == w, occ_ref[slot, w], total)
    on = lax.shift_right_logical(total, bit) & 1
    return jnp.where(inside, on, 0).astype(F32)[:1]


def y_side(dirs, q, receiving):
    if dirs == 1:
        return 1 - lax.axis_index("gy")
    return q if receiving else 1 - q


def send_choices(send_ref, dirs):
    places = slot_places(send_ref)

    def split(row):
        return row >> 6, (row >> 3) & 7, row & 7

    along_x = []
    lane = iota((FACE, FACE), 1)
    for side in (1, 0):
        i, j, l = split(iota((FACE, FACE), 0) + 384 * side)
        ahead = jnp.int32(0)
        picks = []
        for px, py, pz, held in places:
            facing = (px == side).astype(jnp.int32) * held
            at_face = i == 7 * side
            blocks = [
                one_hot(jnp.where(at_face & (facing == 1), ahead * 64 + j * 8 + l, -1) == lane)
            ]
            ahead = ahead + facing
            for q in range(dirs):
                col = y_side(dirs, q, False)
                here = at_face & (j == 7 * col) & ((facing == 1) & (py == col))
                edge = jnp.where(here, 16 * (1 - side) + pz * 8 + l, -1)
                blocks.append(one_hot(edge == (lane & 31)))
            picks.append(jnp.concatenate(blocks, axis=1))
        along_x.append(picks)
    along_y = []
    lane = iota((VOX, FACE), 1)
    i, j, l = split(iota((VOX, FACE), 0))
    for q in range(dirs):
        col = y_side(dirs, q, False)
        ahead = jnp.int32(0)
        picks = []
        for px, py, pz, held in places:
            facing = (py == col).astype(jnp.int32) * held
            here = (j == 7 * col) & (facing == 1)
            picks.append(one_hot(jnp.where(here, ahead * 64 + i * 8 + l, -1) == lane))
            ahead = ahead + facing
        along_y.append(picks)
    return along_x, along_y


def pack_sends(own_ref, send_ref, dirs, plus_ref, minus_ref, y_ref):
    channels = own_ref.shape[1]
    group = channels // 4
    along_x, along_y = send_choices(send_ref, dirs)
    glane = iota((group, FACE), 1) >> 5
    for side, picks, ref in ((1, along_x[0], plus_ref), (0, along_x[1], minus_ref)):
        lanes = slice(384 * side, 384 * side + 128)
        wide = jnp.dot(own_ref[0, :, lanes], picks[0], preferred_element_type=F32) + jnp.dot(
            own_ref[1, :, lanes], picks[1], preferred_element_type=F32
        )
        ref[:channels, :] = wide[:, :FACE].astype(BF)
        for q in range(dirs):
            at = FACE * (1 + q)
            packed = jnp.zeros((group, FACE), F32)
            for g in range(4):
                packed = jnp.where(
                    glane == g, wide[group * g : group * g + group, at : at + FACE], packed
                )
            ref[channels + group * q : channels + group * q + group, :] = packed.astype(BF)
    for q in range(dirs):
        y_ref[q, :, :] = (
            jnp.dot(own_ref[0], along_y[q][0], preferred_element_type=F32)
            + jnp.dot(own_ref[1], along_y[q][1], preferred_element_type=F32)
        ).astype(BF)


def ring_of(x, y):
    return jnp.where(x == 0, y, jnp.where(x == 9, 10 + y, jnp.where(y == 0, 19 + x, 27 + x)))


def encode(x, y, z, ok):
    ok = ok & (x >= 0) & (x <= 9) & (y >= 0) & (y <= 9) & (z >= -1) & (z <= 8)
    side = ring_of(x, y) * 8 + z
    ends = 288 + (x * 10 + y) * 2 + jnp.where(z > 7, 1, 0)
    return jnp.where(ok, jnp.where((z < 0) | (z > 7), ends, side), -1)


def halo_choice(so_ref, sr_ref, n, send_ref, near_ref, dirs):
    places = slot_places(send_ref)
    nx, ny, nz, _ = places[n]
    px, py, pz, _ = places[1 - n]

    def put(ref, at, rows, target):
        for b in range(HALO // 128):
            ref[n, at : at + rows, 128 * b : 128 * b + 128] = one_hot(
                target == iota((rows, 128), 1) + 128 * b
            )

    row = iota((VOX, 128), 0)
    put(
        so_ref,
        0,
        VOX,
        encode(
            (row >> 6) + 1 + 8 * (px - nx),
            ((row >> 3) & 7) + 1 + 8 * (py - ny),
            (row & 7) + 8 * (pz - nz),
            row >= 0,
        ),
    )

    def ranked(offset_of):
        count = jnp.int32(0)
        firsts = [jnp.int32(FAR), jnp.int32(FAR)]
        depths = [jnp.int32(0), jnp.int32(0)]
        for across in range(2):
            for z in range(2):
                there = (near_ref[n, offset_of(across, z)] >= 0).astype(jnp.int32)
                for rank in range(2):
                    take = (there == 1) & (count == rank)
                    firsts[rank] = jnp.where(take, across, firsts[rank])
                    depths[rank] = jnp.where(take, z, depths[rank])
                count = count + there
        return firsts, depths

    row = iota((FACE, 128), 0)
    high = row >= 64
    u = (row >> 3) & 7
    l = row & 7
    nought = jnp.zeros((FACE, 128), jnp.int32)
    firsts, depths = ranked(
        lambda across, z: 18 * nx + 3 * (across - ny + 1) + (z - nz + 1)
    )
    across = jnp.where(high, firsts[1], firsts[0])
    depth = jnp.where(high, depths[1], depths[0])
    for side in range(2):
        put(
            sr_ref,
            FACE * side,
            FACE,
            encode(
                nought + 9 * side,
                u + 1 + 8 * (across - ny),
                l + 8 * (depth - nz),
                nought + nx == side,
            ),
        )
    firsts, depths = ranked(
        lambda across, z: 9 * (across - nx + 1) + 6 * ny + (z - nz + 1)
    )
    across = jnp.where(high, firsts[1], firsts[0])
    depth = jnp.where(high, depths[1], depths[0])
    e = row & 31
    from_side = e >> 4
    for q in range(dirs):
        side = y_side(dirs, q, True)
        put(
            sr_ref,
            FACE * (2 + q),
            FACE,
            encode(
                u + 1 + 8 * (across - nx),
                nought + 9 * side,
                l + 8 * (depth - nz),
                nought + ny == side,
            ),
        )
        put(
            sr_ref,
            FACE * (2 + dirs + q),
            FACE,
            encode(
                9 * from_side,
                nought + 9 * side,
                (e & 7) + 8 * (((e >> 3) & 1) - nz),
                (from_side == nx) & (nought + ny == side),
            ),
        )


def padded_choice(stat_ref):
    lane = iota((8, PADDED), 1)
    x = lax.shift_right_logical(lane * 205, 14)
    rest = lane - x * PLANE
    y = rest >> 3
    l = rest & 7
    within = (x >= 1) & (x <= 8) & (y >= 1) & (y <= 8)
    own = jnp.where(within, (x - 1) * 64 + (y - 1) * 8 + l, -1)
    side = jnp.where(within | (x > 9), -1, ring_of(x, y) * 8 + l)
    ends = jnp.where(
        (x <= 9) & ((l == 0) | (l == 7)), 288 + (x * 10 + y) * 2 + jnp.where(l == 7, 1, 0), -1
    )
    row = iota((HALO, PADDED), 0)
    for index, target in enumerate((own, side, ends)):
        stat_ref[index] = one_hot(row == target[:1])


def fill_padded(own_ref, part_ref, recv_minus, recv_plus, recv_y, sr_ref, stat_ref, d_ref, xh_ref, dirs, outs, ready):
    channels = own_ref.shape[1]
    group = channels // 4
    d_ref[:, :FACE] = recv_minus[:channels, :]
    d_ref[:, FACE : 2 * FACE] = recv_plus[:channels, :]
    glane = iota((group, FACE), 1) >> 5
    for q in range(dirs):
        at = FACE * (2 + q)
        d_ref[:, at : at + FACE] = recv_y[q, :channels, :]
        packed = recv_y[q, channels : channels + group, :].astype(F32)
        spread = jnp.concatenate([jnp.where(glane == g, packed, 0.0) for g in range(4)], axis=0)
        at = FACE * (2 + dirs + q)
        d_ref[:, at : at + FACE] = spread.astype(BF)
    ready(0)
    halos = [jnp.dot(d_ref[...], sr_ref[n], preferred_element_type=F32) for n in range(2)]
    ready(1)
    for n in range(2):
        rows = slice(channels * n, channels * n + channels)
        xh_ref[rows, :VOX] = own_ref[n]
        xh_ref[rows, VOX:] = (halos[n] + part_ref[n].astype(F32)).astype(BF)
    middle = jnp.dot(xh_ref[:, :VOX], stat_ref[0], preferred_element_type=F32) + jnp.dot(
        xh_ref[:, VOX:], stat_ref[1], preferred_element_type=F32
    )
    ends = jnp.dot(xh_ref[:, VOX:], stat_ref[2], preferred_element_type=F32)
    for ref, first, count, flip in outs:
        l = iota((count, PADDED), 1) & 7
        for n in range(2):
            rows = slice(channels * n + first, channels * n + first + count)
            mid = middle[rows]
            end = ends[rows]
            at = slice(PADDED * n, PADDED * n + PADDED)
            below = jnp.where(l == 0, end, pltpu.roll(mid, 1, 1)).astype(BF)
            above = jnp.where(l == 7, end, pltpu.roll(mid, PADDED - 1, 1)).astype(BF)
            low, high = (above, below) if flip else (below, above)
            ref[:count, at] = low
            ref[count : 2 * count, at] = mid.astype(BF)
            ref[2 * count :, at] = high


def fill_patches(p_ref, z_ref):
    for k in range(TAPS):
        a, b, c = k // 9, k // 3 % 3, k % 3
        for n in range(2):
            at = PADDED * n + PLANE * a + 8 * b
            p_ref[96 * k : 96 * k + 96, OUTER * n : OUTER * n + OUTER] = z_ref[
                96 * c : 96 * c + 96, at : at + OUTER
            ]


def shifted_sum(s_ref, n, flip):
    total = None
    for ab in range(9):
        a, b = ab // 3, ab % 3
        if flip:
            a, b = 2 - a, 2 - b
        at = PADDED * n + PLANE * a + 8 * b
        part = s_ref[96 * ab : 96 * ab + 96, at : at + OUTER]
        total = part if total is None else total + part
    return total


def compaction():
    row = iota((OUTER, VOX), 0)
    x = lax.shift_right_logical(row * 205, 14)
    rest = row - x * PLANE
    return one_hot(jnp.where(rest < 64, x * 64 + rest, -1) == iota((OUTER, VOX), 1))


def fetch(pairs, sems):
    copies = [pltpu.make_async_copy(p[0], p[1], sems.at[k]) for k, p in enumerate(pairs)]
    for copy in copies:
        copy.start()
    return copies


def pack_kernel(dirs, feat_ref, cot_ref, occ_ref, send_ref, own_ref, plus_ref, minus_ref, y_ref):
    for n in range(2):
        mask = lane_mask(occ_ref, n, VOX, 64)
        own_ref[n, :96, :] = jnp.where(mask > 0.5, feat_ref[n].astype(F32), 0.0).astype(BF)
        own_ref[n, 96:, :] = jnp.where(mask > 0.5, cot_ref[n].astype(F32), 0.0).astype(BF)
    pack_sends(own_ref, send_ref, dirs, plus_ref, minus_ref, y_ref)


def prepare_kernel(
    dirs, own_ref, near_ref, send_ref, wa_ref,
    so_ref, sr_ref, stat_ref, part_ref, wa9_ref,
):
    for n in range(2):
        halo_choice(so_ref, sr_ref, n, send_ref, near_ref, dirs)
    padded_choice(stat_ref)
    for n in range(2):
        part_ref[n] = jnp.dot(own_ref[1 - n], so_ref[n], preferred_element_type=F32).astype(BF)
    for k in range(TAPS):
        c, ab = k % 3, k // 3
        wa9_ref[96 * ab : 96 * ab + 96, 96 * c : 96 * c + 96] = wa_ref[k].astype(F32).T.astype(BF)


def first_kernel(
    dirs, fm_ref, fp_ref, fy_ref, sr_ref, occ_ref, send_ref, own_ref, part_ref, stat_ref, wa_ref, wb_ref,
    zx_ref, gpre_ref, hid_ref, plus_ref, minus_ref, y_ref,
    d_ref, xh_ref, zg_ref, s9_ref, pre_ref, wb9_ref,
):
    fill_padded(
        own_ref, part_ref, fm_ref, fp_ref, fy_ref, sr_ref, stat_ref, d_ref, xh_ref, dirs,
        ((zx_ref, 0, 96, False), (zg_ref, 96, 256, True)),
        lambda stage: None,
    )
    s9_ref[...] = jnp.dot(wa_ref[...], zx_ref[...], preferred_element_type=F32)
    for n in range(2):
        pre_ref[:, OUTER * n : OUTER * n + OUTER] = shifted_sum(s9_ref, n, False)
    for k in range(TAPS):
        c, ab = k % 3, k // 3
        wb9_ref[96 * ab : 96 * ab + 96, 256 * c : 256 * c + 256] = wb_ref[k]
    s9_ref[...] = jnp.dot(wb9_ref[...], zg_ref[...], preferred_element_type=F32)
    squeeze = compaction()
    for n in range(2):
        at = slice(OUTER * n, OUTER * n + OUTER)
        mask = lane_mask(occ_ref, n, OUTER, PLANE)
        pre = pre_ref[:, at] * mask
        gate = 1.0 / (1.0 + jnp.exp(-pre))
        hidden = (pre * gate).astype(BF)
        grad_pre = (
            shifted_sum(s9_ref, n, True) * gate * (1.0 + pre * (1.0 - gate)) * mask
        ).astype(BF)
        gpre_ref[:, at] = grad_pre
        both = jnp.concatenate([hidden, grad_pre], axis=0)
        hid_ref[n] = jnp.dot(both, squeeze, preferred_element_type=F32).astype(BF)
    pack_sends(hid_ref, send_ref, dirs, plus_ref, minus_ref, y_ref)


def weight_a_kernel(
    scale, zx_ref, gpre_ref, own_ref, stat_ref, hid_ref, so_ref, wb_ref,
    out_hbm, hpart_hbm, gout_hbm, wbt_hbm,
    g9_ref, out_ref, hpart_ref, gout_ref, wbt_ref, sems,
):
    def store(source, target, k):
        copy = pltpu.make_async_copy(source, target, sems.at[k])
        copy.start()
        return copy

    for n in range(2):
        hpart_ref[n] = jnp.dot(hid_ref[1 - n], so_ref[n], preferred_element_type=F32).astype(BF)
        spread = jnp.dot(own_ref[n, 96:, :], stat_ref[0], preferred_element_type=F32)
        gout_ref[:, OUTER * n : OUTER * n + OUTER] = spread[:, FIRST : FIRST + OUTER].astype(BF)
    stores = [store(hpart_ref, hpart_hbm, 0), store(gout_ref, gout_hbm, 1)]
    for k in range(TAPS):
        wbt_ref[:, 96 * k : 96 * k + 96] = wb_ref[k].astype(F32).T.astype(BF)
    stores.append(store(wbt_ref, wbt_hbm, 2))
    g9_ref[...] = jnp.zeros_like(g9_ref)
    for ab in range(9):
        for n in range(2):
            at = PADDED * n + PLANE * (ab // 3) + 8 * (ab % 3)
            g9_ref[128 * ab : 128 * ab + 96, at : at + OUTER] = gpre_ref[
                :, OUTER * n : OUTER * n + OUTER
            ]
    out_ref[...] = jnp.zeros_like(out_ref)
    total = scale * lax.dot_general(
        zx_ref[...], g9_ref[...], NT, preferred_element_type=F32
    )
    for k in range(TAPS):
        half, at = k // 14, 96 * (k % 14)
        c, ab = k % 3, k // 3
        out_ref[half, at : at + 96, :] = total[96 * c : 96 * c + 96, 128 * ab : 128 * ab + 128]
    stores.append(store(out_ref, out_hbm, 3))
    for copy in stores:
        copy.wait()


def weight_b_kernel(
    scale, dirs, split, fm_ref, fp_ref, fy_ref, own_ref, stat_ref,
    sr_hbm, part_hbm, gout_hbm, wa_hbm, zh_hbm, zp_hbm, keep_ref, *rest,
):
    sr_ref, part_ref, gout_ref, wa_ref, zh_ref, zp_ref, d_ref, xh_ref, p_ref, sum_ref, sems = rest[-11:]
    copies = fetch(
        ((sr_hbm, sr_ref), (part_hbm, part_ref), (gout_hbm, gout_ref), (wa_hbm, wa_ref)), sems
    )
    fill_padded(
        own_ref, part_ref, fm_ref, fp_ref, fy_ref, sr_ref, stat_ref, d_ref, xh_ref, dirs,
        ((zh_ref, 0, 96, False), (zp_ref, 96, 96, True)),
        lambda stage: copies[stage].wait(),
    )
    stores = fetch(((zh_ref, zh_hbm), (zp_ref, zp_hbm)), sems.at[pl.ds(4, 2)])
    fill_patches(p_ref, zh_ref)
    copies[2].wait()
    rows = TAPS * 96
    total = scale * lax.dot_general(p_ref[...], gout_ref[...], NT, preferred_element_type=F32)
    copies[3].wait()
    for half in range(2):
        sum_ref[half, :rows, :] = total[:, 128 * half : 128 * half + 128]
        sum_ref[half, rows:STORED, :] = jnp.zeros((STORED - rows, 128), F32)
        sum_ref[half, STORED:, :] = wa_ref[half]
    if split:
        core = lax.axis_index("gx") & 1
        keep = pl.multiple_of(core * (HALF // 2), HALF // 2)
        send = pl.multiple_of((1 - core) * (HALF // 2), HALF // 2)
        keep_ref[...] = sum_ref[:, pl.ds(keep, HALF // 2), :]
        rest[0][...] = sum_ref[:, pl.ds(send, HALF // 2), :].astype(BF)
    else:
        keep_ref[...] = sum_ref[...]
    for store in stores:
        store.wait()


def out_kernel(occ_ref, zh_hbm, wbt_hbm, out_ref, p_ref, zh_ref, wbt_ref, sems):
    copies = fetch(((zh_hbm, zh_ref), (wbt_hbm, wbt_ref)), sems)
    squeeze = compaction()
    copies[0].wait()
    fill_patches(p_ref, zh_ref)
    copies[1].wait()
    total = jnp.dot(wbt_ref[...], p_ref[...], preferred_element_type=F32)
    for n in range(2):
        mask = lane_mask(occ_ref, n, OUTER, PLANE)
        part = total[:, OUTER * n : OUTER * n + OUTER] * mask
        out_ref[n] = jnp.dot(part.astype(BF), squeeze, preferred_element_type=F32).astype(BF)


def grad_kernel(occ_ref, zp_hbm, wa_hbm, grad_ref, s9_ref, wg9_ref, zp_ref, wa_ref, sems):
    copies = fetch(((wa_hbm, wa_ref), (zp_hbm, zp_ref)), sems)
    squeeze = compaction()
    copies[0].wait()
    for k in range(TAPS):
        c, ab = k % 3, k // 3
        wg9_ref[96 * ab : 96 * ab + 96, 96 * c : 96 * c + 96] = wa_ref[k]
    copies[1].wait()
    s9_ref[...] = jnp.dot(wg9_ref[...], zp_ref[...], preferred_element_type=F32)
    for n in range(2):
        mask = lane_mask(occ_ref, n, OUTER, PLANE)
        grad_ref[n] = jnp.dot(
            (shifted_sum(s9_ref, n, True) * mask).astype(BF), squeeze, preferred_element_type=F32
        ).astype(BF)


def unpack_kernel(mine_ref, other_ref, wa_hbm, wb_hbm, all_ref, wa_ref, wb_ref, sems):
    core = lax.axis_index("gx") & 1
    for index, ref in enumerate((mine_ref, other_ref)):
        at = core if index == 0 else 1 - core
        at = pl.multiple_of(at * (HALF // 2), HALF // 2)
        all_ref[:, pl.ds(at, HALF // 2), :] = ref[...]
    copies = []

    def store(source, target):
        copies.append(pltpu.make_async_copy(source, target, sems.at[len(copies)]))
        copies[-1].start()

    for k in range(TAPS):
        for side in range(2):
            wb_ref[k, :, 128 * side : 128 * side + 128] = all_ref[
                side, 96 * k : 96 * k + 96, :
            ].astype(F32)
        if k % 9 == 8:
            store(wb_ref.at[pl.ds(k - 8, 9)], wb_hbm.at[pl.ds(k - 8, 9)])
    for k in range(TAPS):
        half, at = k // 14, STORED + 96 * (k % 14)
        wa_ref[k] = all_ref[half, at : at + 96, :96].astype(F32)
    store(wa_ref, wa_hbm)
    for copy in copies:
        copy.wait()


def call(kernel, outs, ins, scratch=(), flops=0, moved=0, far_ins=0, far_outs=0, sems=0, limit=LIMIT):
    specs = [SMEM if jnp.issubdtype(x.dtype, jnp.integer) else VMEM for x in ins]
    for k in range(far_ins):
        specs[len(ins) - 1 - k] = FAR_SPEC
    out_specs = [VMEM] * len(outs)
    for k in range(far_outs):
        out_specs[k] = FAR_SPEC
    scratch = [pltpu.VMEM(s, d) for s, d in scratch]
    if sems:
        scratch.append(pltpu.SemaphoreType.DMA((sems,)))
    return pl.pallas_call(
        kernel,
        out_shape=[jax.ShapeDtypeStruct(s, d) for s, d in outs],
        in_specs=specs,
        out_specs=out_specs,
        scratch_shapes=scratch,
        compiler_params=pltpu.CompilerParams(vmem_limit_bytes=limit),
        cost_estimate=pl.CostEstimate(flops=flops, bytes_accessed=moved, transcendentals=0),
    )(*ins)


def exchange(channels, plus, minus, faces, count_x, count_y, cover):
    up = [(k, k + 1) for k in range(count_x - 1)]
    down = [(k + 1, k) for k in range(count_x - 1)]
    from_minus = lax.ppermute(plus, "gx", up)
    from_plus = lax.ppermute(minus, "gx", down)
    covered = cover()
    faces, covered = lax.optimization_barrier((faces, covered))
    group = channels // 4
    dirs = faces.shape[0]
    if dirs == 1:
        perms = [[(0, 1), (1, 0)]]
    else:
        perms = [
            [(k, k + 1) for k in range(count_y - 1)],
            [(k + 1, k) for k in range(count_y - 1)],
        ]
    arrived = []
    for q in range(dirs):
        at = channels + group * q
        edges = from_minus[at : at + group] + from_plus[at : at + group]
        arrived.append(
            lax.ppermute(jnp.concatenate([faces[q], edges], axis=0), "gy", perms[q])
        )
    return from_minus, from_plus, jnp.stack(arrived, axis=0), covered


def swap_or_keep(piece, bit):
    rows = piece.shape[0] // 2
    low, high = piece[:rows], piece[rows:]
    return jnp.where(bit == 0, high, low).astype(BF), jnp.where(bit == 0, low, high)


def body(features, occupancy, neighbours, send_slots, weight_a, weight_b, cotangent):
    count_x = lax.axis_size("gx")
    count_y = lax.axis_size("gy")
    dirs = 1 if count_y == 2 else 2
    split = count_x == 4 and count_y == 2
    scale = float(features.shape[0] * VOX * count_x * count_y) ** -0.5
    lanes = FACE * (2 + 2 * dirs)
    wide = 2 * PADDED
    outer = 2 * OUTER

    rows = 352 + 88 * dirs
    own, plus, minus, faces = call(
        functools.partial(pack_kernel, dirs),
        [((2, 352, VOX), BF), ((rows, FACE), BF), ((rows, FACE), BF), ((dirs, 352, FACE), BF)],
        [features, cotangent, occupancy, send_slots],
        flops=352 * 1024 * 1024,
        moved=2 * 1024 * 1024,
    )

    def prepare():
        return call(
            functools.partial(prepare_kernel, dirs),
            [
                ((2, VOX, HALO), BF),
                ((2, lanes, HALO), BF),
                ((3, HALO, PADDED), BF),
                ((2, 352, HALO), BF),
                ((864, 288), BF),
            ],
            [own, neighbours, send_slots, weight_a],
            flops=10**9,
            moved=8 * MIB,
            limit=8 * MIB,
        )

    from_minus, from_plus, from_y, prepared = exchange(
        352, plus, minus, faces, count_x, count_y, prepare
    )
    halo_own, halo_far, padded, part, wa9 = prepared

    rows = 192 + 48 * dirs
    zx, gpre, hid, plus, minus, faces = call(
        functools.partial(first_kernel, dirs),
        [
            ((288, wide), BF),
            ((96, outer), BF),
            ((2, 192, VOX), BF),
            ((rows, FACE), BF),
            ((rows, FACE), BF),
            ((dirs, 192, FACE), BF),
        ],
        [
            from_minus, from_plus, from_y, halo_far, occupancy, send_slots,
            own, part, padded, wa9, weight_b,
        ],
        [
            ((352, lanes), BF),
            ((704, 1024), BF),
            ((768, wide), BF),
            ((864, wide), F32),
            ((96, outer), F32),
            ((864, 768), BF),
        ],
        flops=5 * 10**9,
        moved=8 * MIB,
        limit=20 * MIB,
    )

    def first_weights():
        return call(
            functools.partial(weight_a_kernel, scale),
            [
                ((2, HALF - STORED, 128), F32),
                ((2, 192, HALO), BF),
                ((256, outer), BF),
                ((256, TAPS * 96), BF),
            ],
            [zx, gpre, own, padded, hid, halo_own, weight_b],
            [
                ((9 * 128, wide), BF),
                ((2, HALF - STORED, 128), F32),
                ((2, 192, HALO), BF),
                ((256, outer), BF),
                ((256, TAPS * 96), BF),
            ],
            flops=2 * 10**9,
            moved=6 * MIB,
            far_outs=4,
            sems=4,
            limit=20 * MIB,
        )

    from_minus, from_plus, from_y, covered = exchange(
        192, plus, minus, faces, count_x, count_y, first_weights
    )
    grad_wa, hpart, gout, wbt = covered
    sums = [((2, HALF, 128), F32)]
    if split:
        sums = [((2, HALF // 2, 128), F32), ((2, HALF // 2, 128), BF)]
    zh, zp, *sums = call(
        functools.partial(weight_b_kernel, scale, dirs, split),
        [((288, wide), BF), ((288, wide), BF)] + sums,
        [from_minus, from_plus, from_y, hid, padded, halo_far, hpart, gout, grad_wa],
        [
            ((2, lanes, HALO), BF),
            ((2, 192, HALO), BF),
            ((256, outer), BF),
            ((2, HALF - STORED, 128), F32),
            ((288, wide), BF),
            ((288, wide), BF),
            ((192, lanes), BF),
            ((384, 1024), BF),
            ((TAPS * 96, outer), BF),
            ((2, HALF, 128), F32),
        ],
        flops=2 * 10**9,
        moved=4 * MIB,
        far_ins=4,
        far_outs=2,
        sems=6,
        limit=22 * MIB,
    )

    def layer(zh):
        return call(
            out_kernel,
            [((2, 256, VOX), BF)],
            [occupancy, zh, wbt],
            [((TAPS * 96, outer), BF), ((288, wide), BF), ((256, TAPS * 96), BF)],
            flops=2 * 10**9,
            moved=3 * MIB,
            far_ins=2,
            sems=2,
            limit=20 * MIB,
        )[0]

    def data_grad(zp):
        return call(
            grad_kernel,
            [((2, 96, VOX), BF)],
            [occupancy, zp, weight_a],
            [((864, wide), F32), ((864, 288), BF), ((288, wide), BF), ((TAPS, 96, 96), BF)],
            flops=2 * 10**9,
            moved=2 * MIB,
            far_ins=2,
            sems=2,
            limit=20 * MIB,
        )[0]

    if not split:
        total = lax.psum(sums[0], ("gx", "gy"))
        grad_wb = jnp.concatenate([total[0, : TAPS * 96], total[1, : TAPS * 96]], axis=1)
        first = total[0, STORED : STORED + 14 * 96, :96]
        second = total[1, STORED : STORED + 13 * 96, :96]
        grad_wa = jnp.concatenate([first, second], axis=0)
        return layer(zh), data_grad(zp), grad_wa.reshape(TAPS, 96, 96), grad_wb.reshape(TAPS, 96, 256)

    along_y = ("gx", [(k, k ^ 2) for k in range(4)])
    along_x = ("gy", [(0, 1), (1, 0)])
    bit_y = lax.axis_index("gx") >> 1
    bit_x = lax.axis_index("gy")
    swap = ("gx", [(k, k ^ 1) for k in range(4)])
    keep, send = sums
    summed = keep + lax.ppermute(send, *swap).astype(F32)
    send_a, keep_a = swap_or_keep(summed[0], bit_y)
    send_b, keep_b = swap_or_keep(summed[1], bit_x)
    zh, send_a, send_b = lax.optimization_barrier((zh, send_a, send_b))
    got_a = lax.ppermute(send_a, *along_y)
    got_b = lax.ppermute(send_b, *along_x)
    layer_out = layer(zh)
    got_a, got_b, layer_out = lax.optimization_barrier((got_a, got_b, layer_out))
    half_a = keep_a + got_a.astype(F32)
    half_b = keep_b + got_b.astype(F32)
    send_a, keep_a = swap_or_keep(half_a, bit_x)
    send_b, keep_b = swap_or_keep(half_b, bit_y)
    got_a = lax.ppermute(send_a, *along_x)
    got_b = lax.ppermute(send_b, *along_y)
    part_a = (keep_a + got_a.astype(F32)).astype(BF)
    part_b = (keep_b + got_b.astype(F32)).astype(BF)

    def joined(piece, other, bit):
        first = bit == 0
        return jnp.concatenate(
            [jnp.where(first, piece, other), jnp.where(first, other, piece)], axis=0
        )

    part_a, part_b = (
        joined(part_a, lax.ppermute(part_a, *along_x), bit_x),
        joined(part_b, lax.ppermute(part_b, *along_y), bit_y),
    )
    zp, part_a, part_b = lax.optimization_barrier((zp, part_a, part_b))
    other_a = lax.ppermute(part_a, *along_y)
    other_b = lax.ppermute(part_b, *along_x)
    grad_features = data_grad(zp)
    other_a, other_b, grad_features = lax.optimization_barrier((other_a, other_b, grad_features))
    mine = jnp.stack([joined(part_a, other_a, bit_y), joined(part_b, other_b, bit_x)], axis=0)
    other = lax.ppermute(mine, *swap)
    grad_wa, grad_wb = call(
        unpack_kernel,
        [((TAPS, 96, 96), F32), ((TAPS, 96, 256), F32)],
        [mine, other],
        [((2, HALF, 128), BF), ((TAPS, 96, 96), F32), ((TAPS, 96, 256), F32)],
        moved=6 * MIB,
        far_outs=2,
        sems=4,
        limit=20 * MIB,
    )
    return layer_out, grad_features, grad_wa, grad_wb


def solution(mesh):
    in_specs = (
        P(("dp", "gx", "gy"), None, None),
        P(("dp", "gx", "gy"), None),
        P(("dp", "gx", "gy"), None),
        P(("dp", "gx"), "gy", None),
        P(),
        P(),
        P(("dp", "gx", "gy"), None, None),
    )
    out_specs = (
        P(("dp", "gx", "gy"), None, None),
        P(("dp", "gx", "gy"), None, None),
        P("dp", None, None),
        P("dp", None, None),
    )
    return jax.shard_map(body, mesh=mesh, in_specs=in_specs, out_specs=out_specs, check_vma=False)
```

```python
import functools

import jax
import jax.numpy as jnp
from jax import lax
from jax.experimental import pallas as pl
from jax.experimental.pallas import tpu as pltpu
from jax.sharding import PartitionSpec as P

EDGE = 8
VOX = 512
TAPS = 27
PLANE = 80
PADDED = 896
OUTER = 640
FIRST = 88
FACE = 128
FAR = 100
HALO = 512
HALF = 4096
STORED = 2688
NT = (((1,), (1,)), ((), ()))
BF = jnp.bfloat16
F32 = jnp.float32
VMEM = pl.BlockSpec(memory_space=pltpu.VMEM)
FAR_SPEC = pl.BlockSpec(memory_space=pltpu.HBM)
SMEM = pl.BlockSpec(memory_space=pltpu.SMEM)
LIMIT = 58 * 1024 * 1024
MIB = 1024 * 1024


def iota(shape, dim):
    return lax.broadcasted_iota(jnp.int32, shape, dim)


def one_hot(cond):
    return jnp.where(cond, 1.0, 0.0).astype(BF)


def slot_places(send_ref):
    places = []
    for slot in range(2):
        px = py = pz = held = jnp.int32(0)
        for x in range(2):
            for y in range(2):
                for z in range(2):
                    here = (send_ref[x, y, z] == slot).astype(jnp.int32)
                    held = held + here
                    px = px + here * x
                    py = py + here * y
                    pz = pz + here * z
        places.append((px, py, pz, held))
    return places


def lane_mask(occ_ref, slot, width, plane):
    lane = iota((8, width), 1)
    if plane == 64:
        voxel = lane
        inside = lane >= 0
    else:
        x = lax.shift_right_logical(lane * 205, 14)
        rest = lane - x * plane
        voxel = x * 64 + rest
        inside = rest < 64
    word = lax.shift_right_logical(voxel * 2185, 16)
    bit = voxel - word * 30
    total = jnp.zeros((8, width), jnp.int32)
    for w in range(18):
        total = jnp.where(word == w, occ_ref[slot, w], total)
    on = lax.shift_right_logical(total, bit) & 1
    return jnp.where(inside, on, 0).astype(F32)[:1]


def y_side(dirs, q, receiving):
    if dirs == 1:
        return 1 - lax.axis_index("gy")
    return q if receiving else 1 - q


def x_side(which):
    odd = lax.axis_index("gx") & 1
    return odd if which else 1 - odd


def send_choices(send_ref, dirs):
    places = slot_places(send_ref)

    def split(row):
        return row >> 6, (row >> 3) & 7, row & 7

    along_x = []
    lane = iota((FACE, FACE), 1)
    for which in range(2):
        side = x_side(which)
        i, j, l = split(iota((FACE, FACE), 0) + 384 * side)
        ahead = jnp.int32(0)
        picks = []
        for px, py, pz, held in places:
            facing = (px == side).astype(jnp.int32) * held
            at_face = i == 7 * side
            blocks = [
                one_hot(jnp.where(at_face & (facing == 1), ahead * 64 + j * 8 + l, -1) == lane)
            ]
            ahead = ahead + facing
            for q in range(dirs):
                col = y_side(dirs, q, False)
                here = at_face & (j == 7 * col) & ((facing == 1) & (py == col))
                edge = jnp.where(here, 16 * (1 - side) + pz * 8 + l, -1)
                blocks.append(one_hot(edge == (lane & 31)))
            picks.append(jnp.concatenate(blocks, axis=1))
        along_x.append(picks)
    along_y = []
    lane = iota((VOX, FACE), 1)
    i, j, l = split(iota((VOX, FACE), 0))
    for q in range(dirs):
        col = y_side(dirs, q, False)
        ahead = jnp.int32(0)
        picks = []
        for px, py, pz, held in places:
            facing = (py == col).astype(jnp.int32) * held
            here = (j == 7 * col) & (facing == 1)
            picks.append(one_hot(jnp.where(here, ahead * 64 + i * 8 + l, -1) == lane))
            ahead = ahead + facing
        along_y.append(picks)
    return along_x, along_y


def pack_sends(own_ref, send_ref, dirs, one_ref, two_ref, y_ref):
    channels = own_ref.shape[1]
    group = channels // 4
    along_x, along_y = send_choices(send_ref, dirs)
    glane = iota((group, FACE), 1) >> 5
    for which, (picks, ref) in enumerate(zip(along_x, (one_ref, two_ref))):
        lanes = pl.ds(pl.multiple_of(384 * x_side(which), 128), 128)
        wide = jnp.dot(own_ref[0, :, lanes], picks[0], preferred_element_type=F32) + jnp.dot(
            own_ref[1, :, lanes], picks[1], preferred_element_type=F32
        )
        ref[:channels, :] = wide[:, :FACE].astype(BF)
        for q in range(dirs):
            at = FACE * (1 + q)
            packed = jnp.zeros((group, FACE), F32)
            for g in range(4):
                packed = jnp.where(
                    glane == g, wide[group * g : group * g + group, at : at + FACE], packed
                )
            ref[channels + group * q : channels + group * q + group, :] = packed.astype(BF)
    for q in range(dirs):
        y_ref[q, :, :] = (
            jnp.dot(own_ref[0], along_y[q][0], preferred_element_type=F32)
            + jnp.dot(own_ref[1], along_y[q][1], preferred_element_type=F32)
        ).astype(BF)


def ring_of(x, y):
    return jnp.where(x == 0, y, jnp.where(x == 9, 10 + y, jnp.where(y == 0, 19 + x, 27 + x)))


def encode(x, y, z, ok):
    ok = ok & (x >= 0) & (x <= 9) & (y >= 0) & (y <= 9) & (z >= -1) & (z <= 8)
    side = ring_of(x, y) * 8 + z
    ends = 288 + (x * 10 + y) * 2 + jnp.where(z > 7, 1, 0)
    return jnp.where(ok, jnp.where((z < 0) | (z > 7), ends, side), -1)


def halo_choice(so_ref, sr_ref, n, send_ref, near_ref, dirs):
    places = slot_places(send_ref)
    nx, ny, nz, _ = places[n]
    px, py, pz, _ = places[1 - n]

    def put(ref, at, rows, target):
        for b in range(HALO // 128):
            ref[n, at : at + rows, 128 * b : 128 * b + 128] = one_hot(
                target == iota((rows, 128), 1) + 128 * b
            )

    row = iota((VOX, 128), 0)
    put(
        so_ref,
        0,
        VOX,
        encode(
            (row >> 6) + 1 + 8 * (px - nx),
            ((row >> 3) & 7) + 1 + 8 * (py - ny),
            (row & 7) + 8 * (pz - nz),
            row >= 0,
        ),
    )

    def ranked(offset_of):
        count = jnp.int32(0)
        firsts = [jnp.int32(FAR), jnp.int32(FAR)]
        depths = [jnp.int32(0), jnp.int32(0)]
        for across in range(2):
            for z in range(2):
                there = (near_ref[n, offset_of(across, z)] >= 0).astype(jnp.int32)
                for rank in range(2):
                    take = (there == 1) & (count == rank)
                    firsts[rank] = jnp.where(take, across, firsts[rank])
                    depths[rank] = jnp.where(take, z, depths[rank])
                count = count + there
        return firsts, depths

    row = iota((FACE, 128), 0)
    high = row >= 64
    u = (row >> 3) & 7
    l = row & 7
    nought = jnp.zeros((FACE, 128), jnp.int32)
    firsts, depths = ranked(
        lambda across, z: 18 * nx + 3 * (across - ny + 1) + (z - nz + 1)
    )
    across = jnp.where(high, firsts[1], firsts[0])
    depth = jnp.where(high, depths[1], depths[0])
    for which in range(2):
        side = x_side(which)
        put(
            sr_ref,
            FACE * which,
            FACE,
            encode(
                nought + 9 * side,
                u + 1 + 8 * (across - ny),
                l + 8 * (depth - nz),
                nought + nx == side,
            ),
        )
    firsts, depths = ranked(
        lambda across, z: 9 * (across - nx + 1) + 6 * ny + (z - nz + 1)
    )
    across = jnp.where(high, firsts[1], firsts[0])
    depth = jnp.where(high, depths[1], depths[0])
    e = row & 31
    from_side = e >> 4
    for q in range(dirs):
        side = y_side(dirs, q, True)
        put(
            sr_ref,
            FACE * (2 + q),
            FACE,
            encode(
                u + 1 + 8 * (across - nx),
                nought + 9 * side,
                l + 8 * (depth - nz),
                nought + ny == side,
            ),
        )
        put(
            sr_ref,
            FACE * (2 + dirs + q),
            FACE,
            encode(
                9 * from_side,
                nought + 9 * side,
                (e & 7) + 8 * (((e >> 3) & 1) - nz),
                (from_side == nx) & (nought + ny == side),
            ),
        )


def padded_choice(stat_ref):
    lane = iota((8, PADDED), 1)
    x = lax.shift_right_logical(lane * 205, 14)
    rest = lane - x * PLANE
    y = rest >> 3
    l = rest & 7
    within = (x >= 1) & (x <= 8) & (y >= 1) & (y <= 8)
    own = jnp.where(within, (x - 1) * 64 + (y - 1) * 8 + l, -1)
    side = jnp.where(within | (x > 9), -1, ring_of(x, y) * 8 + l)
    ends = jnp.where(
        (x <= 9) & ((l == 0) | (l == 7)), 288 + (x * 10 + y) * 2 + jnp.where(l == 7, 1, 0), -1
    )
    row = iota((HALO, PADDED), 0)
    for index, target in enumerate((own, side, ends)):
        stat_ref[index] = one_hot(row == target[:1])


def fill_padded(own_ref, part_ref, recv_one, recv_two, recv_y, sr_ref, stat_ref, d_ref, xh_ref, dirs, outs):
    channels = own_ref.shape[1]
    group = channels // 4
    d_ref[:, :FACE] = recv_one[:channels, :]
    d_ref[:, FACE : 2 * FACE] = recv_two[:channels, :]
    glane = iota((group, FACE), 1) >> 5
    for q in range(dirs):
        at = FACE * (2 + q)
        d_ref[:, at : at + FACE] = recv_y[q, :channels, :]
        packed = recv_y[q, channels : channels + group, :].astype(F32)
        spread = jnp.concatenate([jnp.where(glane == g, packed, 0.0) for g in range(4)], axis=0)
        at = FACE * (2 + dirs + q)
        d_ref[:, at : at + FACE] = spread.astype(BF)
    halos = [jnp.dot(d_ref[...], sr_ref[n], preferred_element_type=F32) for n in range(2)]
    for n in range(2):
        rows = slice(channels * n, channels * n + channels)
        xh_ref[rows, :VOX] = own_ref[n]
        xh_ref[rows, VOX:] = (halos[n] + part_ref[n].astype(F32)).astype(BF)
    middle = jnp.dot(xh_ref[:, :VOX], stat_ref[0], preferred_element_type=F32) + jnp.dot(
        xh_ref[:, VOX:], stat_ref[1], preferred_element_type=F32
    )
    ends = jnp.dot(xh_ref[:, VOX:], stat_ref[2], preferred_element_type=F32)
    for ref, first, count, flip in outs:
        l = iota((count, PADDED), 1) & 7
        for n in range(2):
            rows = slice(channels * n + first, channels * n + first + count)
            mid = middle[rows]
            end = ends[rows]
            at = slice(PADDED * n, PADDED * n + PADDED)
            below = jnp.where(l == 0, end, pltpu.roll(mid, 1, 1)).astype(BF)
            above = jnp.where(l == 7, end, pltpu.roll(mid, PADDED - 1, 1)).astype(BF)
            low, high = (above, below) if flip else (below, above)
            ref[:count, at] = low
            ref[count : 2 * count, at] = mid.astype(BF)
            ref[2 * count :, at] = high


def shifted_sum(s_ref, n, flip):
    total = None
    for ab in range(9):
        a, b = ab // 3, ab % 3
        if flip:
            a, b = 2 - a, 2 - b
        at = PADDED * n + PLANE * a + 8 * b
        part = s_ref[96 * ab : 96 * ab + 96, at : at + OUTER]
        total = part if total is None else total + part
    return total


def compaction():
    row = iota((OUTER, VOX), 0)
    x = lax.shift_right_logical(row * 205, 14)
    rest = row - x * PLANE
    return one_hot(jnp.where(rest < 64, x * 64 + rest, -1) == iota((OUTER, VOX), 1))


def fetch(pairs, sems):
    copies = [pltpu.make_async_copy(p[0], p[1], sems.at[k]) for k, p in enumerate(pairs)]
    for copy in copies:
        copy.start()
    return copies


def pack_kernel(dirs, feat_ref, cot_ref, occ_ref, send_ref, own_ref, one_ref, two_ref, y_ref):
    for n in range(2):
        mask = lane_mask(occ_ref, n, VOX, 64)
        own_ref[n, :96, :] = jnp.where(mask > 0.5, feat_ref[n].astype(F32), 0.0).astype(BF)
        own_ref[n, 96:, :] = jnp.where(mask > 0.5, cot_ref[n].astype(F32), 0.0).astype(BF)
    pack_sends(own_ref, send_ref, dirs, one_ref, two_ref, y_ref)


def halo_kernel(dirs, own_ref, near_ref, send_ref, so_ref, sr_ref, part_ref):
    for n in range(2):
        halo_choice(so_ref, sr_ref, n, send_ref, near_ref, dirs)
    for n in range(2):
        part_ref[n] = jnp.dot(own_ref[1 - n], so_ref[n], preferred_element_type=F32).astype(BF)


def layout_kernel(wa_ref, wb_ref, stat_ref, wa9_ref, wbt_ref):
    padded_choice(stat_ref)
    for k in range(TAPS):
        c, ab = k % 3, k // 3
        wa9_ref[96 * ab : 96 * ab + 96, 96 * c : 96 * c + 96] = wa_ref[k].astype(F32).T.astype(BF)
        wbt_ref[:, 96 * k : 96 * k + 96] = wb_ref[k].astype(F32).T.astype(BF)


def first_kernel(
    dirs, f1_ref, f2_ref, fy_ref, sr_ref, occ_ref, send_ref, own_ref, part_ref, stat_ref, wa_ref, wb_ref,
    zx_ref, zg_ref, gpre_ref, wide_ref, hid_ref, one_ref, two_ref, y_ref,
    d_ref, xh_ref, s9_ref, pre_ref, wb9_ref,
):
    fill_padded(
        own_ref, part_ref, f1_ref, f2_ref, fy_ref, sr_ref, stat_ref, d_ref, xh_ref, dirs,
        ((zx_ref, 0, 96, False), (zg_ref, 96, 256, True)),
    )
    s9_ref[...] = jnp.dot(wa_ref[...], zx_ref[...], preferred_element_type=F32)
    for n in range(2):
        pre_ref[:, OUTER * n : OUTER * n + OUTER] = shifted_sum(s9_ref, n, False)
    for k in range(TAPS):
        c, ab = k % 3, k // 3
        wb9_ref[96 * ab : 96 * ab + 96, 256 * c : 256 * c + 256] = wb_ref[k]
    s9_ref[...] = jnp.dot(wb9_ref[...], zg_ref[...], preferred_element_type=F32)
    squeeze = compaction()
    for n in range(2):
        at = slice(OUTER * n, OUTER * n + OUTER)
        mask = lane_mask(occ_ref, n, OUTER, PLANE)
        pre = pre_ref[:, at] * mask
        gate = 1.0 / (1.0 + jnp.exp(-pre))
        hidden = (pre * gate).astype(BF)
        grad_pre = (
            shifted_sum(s9_ref, n, True) * gate * (1.0 + pre * (1.0 - gate)) * mask
        ).astype(BF)
        gpre_ref[:, at] = grad_pre
        wide_ref[:, at] = hidden
        both = jnp.concatenate([hidden, grad_pre], axis=0)
        hid_ref[n] = jnp.dot(both, squeeze, preferred_element_type=F32).astype(BF)
    pack_sends(hid_ref, send_ref, dirs, one_ref, two_ref, y_ref)


def weights_kernel(scale, split, zx_ref, zg_ref, gpre_ref, wide_ref, keep_ref, *rest):
    g9_ref, h9_ref, sum_ref = rest[-3:]
    h9_ref[...] = jnp.zeros_like(h9_ref)
    g9_ref[...] = jnp.zeros_like(g9_ref)
    for ab in range(9):
        for n in range(2):
            own = slice(OUTER * n, OUTER * n + OUTER)
            at = PADDED * n + PLANE * (2 - ab // 3) + 8 * (2 - ab % 3)
            h9_ref[96 * ab : 96 * ab + 96, at : at + OUTER] = wide_ref[:, own]
            at = PADDED * n + PLANE * (ab // 3) + 8 * (ab % 3)
            g9_ref[128 * ab : 128 * ab + 96, at : at + OUTER] = gpre_ref[:, own]
    total = scale * lax.dot_general(h9_ref[...], zg_ref[...], NT, preferred_element_type=F32)
    rows = TAPS * 96
    sum_ref[:, rows:STORED, :] = jnp.zeros((2, STORED - rows, 128), F32)
    sum_ref[:, STORED + 14 * 96 :, :] = jnp.zeros((2, HALF - STORED - 14 * 96, 128), F32)
    sum_ref[1, STORED + 13 * 96 : STORED + 14 * 96, :] = jnp.zeros((96, 128), F32)
    for k in range(TAPS):
        c, ab = k % 3, k // 3
        for half in range(2):
            sum_ref[half, 96 * k : 96 * k + 96, :] = total[
                96 * ab : 96 * ab + 96, 256 * c + 128 * half : 256 * c + 128 * half + 128
            ]
    total = scale * lax.dot_general(zx_ref[...], g9_ref[...], NT, preferred_element_type=F32)
    for k in range(TAPS):
        half, at = k // 14, STORED + 96 * (k % 14)
        c, ab = k % 3, k // 3
        sum_ref[half, at : at + 96, :] = total[96 * c : 96 * c + 96, 128 * ab : 128 * ab + 128]
    if split:
        core = lax.axis_index("gx") & 1
        keep = pl.multiple_of(core * (HALF // 2), HALF // 2)
        send = pl.multiple_of((1 - core) * (HALF // 2), HALF // 2)
        keep_ref[...] = sum_ref[:, pl.ds(keep, HALF // 2), :]
        rest[0][...] = sum_ref[:, pl.ds(send, HALF // 2), :].astype(BF)
    else:
        keep_ref[...] = sum_ref[...]


def second_kernel(
    dirs, f1_ref, f2_ref, fy_ref, sr_ref, so_ref, own_ref, stat_ref, zh_ref, zp_ref, d_ref, xh_ref, part_ref
):
    for n in range(2):
        part_ref[n] = jnp.dot(own_ref[1 - n], so_ref[n], preferred_element_type=F32).astype(BF)
    fill_padded(
        own_ref, part_ref, f1_ref, f2_ref, fy_ref, sr_ref, stat_ref, d_ref, xh_ref, dirs,
        ((zh_ref, 0, 96, False), (zp_ref, 96, 96, True)),
    )


def out_kernel(n, occ_ref, zh_hbm, wbt_hbm, *rest):
    out_hbm, p_ref, zh_ref, wbt_ref, out_ref, sems = rest[-6:]
    lanes = pl.ds(PADDED * n, PADDED)
    copies = fetch(((zh_hbm.at[:, lanes], zh_ref), (wbt_hbm, wbt_ref)), sems)
    squeeze = compaction()
    copies[0].wait()
    for k in range(TAPS):
        a, b, c = k // 9, k // 3 % 3, k % 3
        at = PLANE * a + 8 * b
        p_ref[96 * k : 96 * k + 96, :] = zh_ref[96 * c : 96 * c + 96, at : at + OUTER]
    copies[1].wait()
    total = jnp.dot(wbt_ref[...], p_ref[...], preferred_element_type=F32)
    total = (total * lane_mask(occ_ref, n, OUTER, PLANE)).astype(BF)
    out_ref[...] = jnp.dot(total, squeeze, preferred_element_type=F32).astype(BF)
    store = pltpu.make_async_copy(out_ref, out_hbm.at[n], sems.at[2])
    store.start()
    store.wait()


def grad_kernel(occ_ref, zp_hbm, wa_hbm, grad_ref, s9_ref, wg9_ref, zp_ref, wa_ref, sems):
    copies = fetch(((wa_hbm, wa_ref), (zp_hbm, zp_ref)), sems)
    squeeze = compaction()
    copies[0].wait()
    for k in range(TAPS):
        c, ab = k % 3, k // 3
        wg9_ref[96 * ab : 96 * ab + 96, 96 * c : 96 * c + 96] = wa_ref[k]
    copies[1].wait()
    s9_ref[...] = jnp.dot(wg9_ref[...], zp_ref[...], preferred_element_type=F32)
    for n in range(2):
        mask = lane_mask(occ_ref, n, OUTER, PLANE)
        grad_ref[n] = jnp.dot(
            (shifted_sum(s9_ref, n, True) * mask).astype(BF), squeeze, preferred_element_type=F32
        ).astype(BF)


def unpack_kernel(mine_ref, other_ref, wa_hbm, wb_hbm, all_ref, wa_ref, wb_ref, sems):
    core = lax.axis_index("gx") & 1
    for index, ref in enumerate((mine_ref, other_ref)):
        at = core if index == 0 else 1 - core
        at = pl.multiple_of(at * (HALF // 2), HALF // 2)
        all_ref[:, pl.ds(at, HALF // 2), :] = ref[...]
    copies = []

    def store(source, target):
        copies.append(pltpu.make_async_copy(source, target, sems.at[len(copies)]))
        copies[-1].start()

    for k in range(TAPS):
        for side in range(2):
            wb_ref[k, :, 128 * side : 128 * side + 128] = all_ref[
                side, 96 * k : 96 * k + 96, :
            ].astype(F32)
        if k % 9 == 8:
            store(wb_ref.at[pl.ds(k - 8, 9)], wb_hbm.at[pl.ds(k - 8, 9)])
    for k in range(TAPS):
        half, at = k // 14, STORED + 96 * (k % 14)
        wa_ref[k] = all_ref[half, at : at + 96, :96].astype(F32)
    store(wa_ref, wa_hbm)
    for copy in copies:
        copy.wait()


def call(kernel, outs, ins, scratch=(), flops=0, moved=0, far_ins=0, far_outs=0, sems=0, limit=LIMIT, aliases={}):
    specs = [SMEM if jnp.issubdtype(x.dtype, jnp.integer) else VMEM for x in ins]
    for k in range(far_ins):
        specs[len(ins) - 1 - k] = FAR_SPEC
    out_specs = [VMEM] * len(outs)
    for k in range(far_outs):
        out_specs[k] = FAR_SPEC
    scratch = [pltpu.VMEM(s, d) for s, d in scratch]
    if sems:
        scratch.append(pltpu.SemaphoreType.DMA((sems,)))
    return pl.pallas_call(
        kernel,
        out_shape=[jax.ShapeDtypeStruct(s, d) for s, d in outs],
        in_specs=specs,
        out_specs=out_specs,
        scratch_shapes=scratch,
        input_output_aliases=aliases,
        compiler_params=pltpu.CompilerParams(vmem_limit_bytes=limit),
        cost_estimate=pl.CostEstimate(flops=flops, bytes_accessed=moved, transcendentals=0),
    )(*ins)


def exchange_x(one, two, count_x):
    def pairs(first):
        starts = range(first, count_x - 1, 2)
        return [(k, k + 1) for k in starts] + [(k + 1, k) for k in starts]

    return lax.ppermute(one, "gx", pairs(0)), lax.ppermute(two, "gx", pairs(1))


def exchange_y(channels, faces, from_one, from_two, count_y):
    group = channels // 4
    dirs = faces.shape[0]
    if dirs == 1:
        perms = [[(0, 1), (1, 0)]]
    else:
        perms = [
            [(k, k + 1) for k in range(count_y - 1)],
            [(k + 1, k) for k in range(count_y - 1)],
        ]
    arrived = []
    for q in range(dirs):
        at = channels + group * q
        edges = from_one[at : at + group] + from_two[at : at + group]
        arrived.append(
            lax.ppermute(jnp.concatenate([faces[q], edges], axis=0), "gy", perms[q])
        )
    return jnp.stack(arrived, axis=0)


def half_rows(piece, which):
    rows = piece.shape[0] // 2
    return lax.dynamic_slice_in_dim(piece, which * rows, rows, axis=0)


def swap_or_keep(piece, bit):
    rows = piece.shape[0] // 2
    low, high = piece[:rows], piece[rows:]
    return jnp.where(bit == 0, high, low).astype(BF), jnp.where(bit == 0, low, high)


def half_sum(kept, got, which):
    return half_rows(kept, which) + half_rows(got, which).astype(F32)


def body(features, occupancy, neighbours, send_slots, weight_a, weight_b, cotangent):
    count_x = lax.axis_size("gx")
    count_y = lax.axis_size("gy")
    dirs = 1 if count_y == 2 else 2
    split = count_x == 4 and count_y == 2
    scale = float(features.shape[0] * VOX * count_x * count_y) ** -0.5
    lanes = FACE * (2 + 2 * dirs)
    wide = 2 * PADDED
    outer = 2 * OUTER

    rows = 352 + 88 * dirs
    own, one, two, faces = call(
        functools.partial(pack_kernel, dirs),
        [((2, 352, VOX), BF), ((rows, FACE), BF), ((rows, FACE), BF), ((dirs, 352, FACE), BF)],
        [features, cotangent, occupancy, send_slots],
        flops=352 * 1024 * 1024,
        moved=2 * 1024 * 1024,
    )

    from_one, from_two = exchange_x(one, two, count_x)
    halo_own, halo_far, part = call(
        functools.partial(halo_kernel, dirs),
        [((2, VOX, HALO), BF), ((2, lanes, HALO), BF), ((2, 352, HALO), BF)],
        [own, neighbours, send_slots],
        flops=10**9,
        moved=4 * MIB,
    )
    faces, part = lax.optimization_barrier((faces, part))
    from_y = exchange_y(352, faces, from_one, from_two, count_y)
    weight_a, weight_b, part = lax.optimization_barrier((weight_a, weight_b, part))
    padded, wa9, wbt = call(
        layout_kernel,
        [((3, HALO, PADDED), BF), ((864, 288), BF), ((256, TAPS * 96), BF)],
        [weight_a, weight_b],
        moved=6 * MIB,
        flops=10**8,
        limit=8 * MIB,
    )
    from_y, padded = lax.optimization_barrier((from_y, padded))

    rows = 192 + 48 * dirs
    zx, zg, gpre, hidden, hid, one, two, faces = call(
        functools.partial(first_kernel, dirs),
        [
            ((288, wide), BF),
            ((768, wide), BF),
            ((96, outer), BF),
            ((96, outer), BF),
            ((2, 192, VOX), BF),
            ((rows, FACE), BF),
            ((rows, FACE), BF),
            ((dirs, 192, FACE), BF),
        ],
        [
            from_one, from_two, from_y, halo_far, occupancy, send_slots,
            own, part, padded, wa9, weight_b,
        ],
        [
            ((352, lanes), BF),
            ((704, 1024), BF),
            ((864, wide), F32),
            ((96, outer), F32),
            ((864, 768), BF),
        ],
        flops=5 * 10**9,
        moved=8 * MIB,
        limit=20 * MIB,
    )
    from_one, from_two = exchange_x(one, two, count_x)
    sums = [((2, HALF, 128), F32)]
    if split:
        sums = [((2, HALF // 2, 128), F32), ((2, HALF // 2, 128), BF)]
    sums = call(
        functools.partial(weights_kernel, scale, split),
        sums,
        [zx, zg, gpre, hidden],
        [((9 * 128, wide), BF), ((9 * 96, wide), BF), ((2, HALF, 128), F32)],
        flops=5 * 10**9,
        moved=6 * MIB,
        limit=24 * MIB,
    )

    from_one, from_two, sums = lax.optimization_barrier((from_one, from_two, sums))
    from_y = exchange_y(192, faces, from_one, from_two, count_y)

    def second(from_one, from_two, from_y):
        return call(
            functools.partial(second_kernel, dirs),
            [((288, wide), BF), ((288, wide), BF)],
            [from_one, from_two, from_y, halo_far, halo_own, hid, padded],
            [((192, lanes), BF), ((384, 1024), BF), ((2, 192, HALO), BF)],
            flops=2 * 10**9,
            moved=6 * MIB,
            limit=14 * MIB,
        )

    def layer(n, zh, wbt, *earlier):
        return call(
            functools.partial(out_kernel, n),
            [((2, 256, VOX), BF)],
            [occupancy, zh, wbt, *earlier],
            [((TAPS * 96, OUTER), BF), ((288, PADDED), BF), ((256, TAPS * 96), BF), ((256, VOX), BF)],
            flops=10**9,
            moved=2 * MIB,
            far_ins=2 + len(earlier),
            far_outs=1,
            sems=3,
            limit=14 * MIB,
            aliases={3: 0} if earlier else {},
        )[0]

    def data_grad(zp):
        return call(
            grad_kernel,
            [((2, 96, VOX), BF)],
            [occupancy, zp, weight_a],
            [((864, wide), F32), ((864, 288), BF), ((288, wide), BF), ((TAPS, 96, 96), BF)],
            flops=2 * 10**9,
            moved=2 * MIB,
            far_ins=2,
            sems=2,
            limit=20 * MIB,
        )[0]

    if not split:
        zh, zp = second(from_one, from_two, from_y)
        total = lax.psum(sums[0], ("gx", "gy"))
        grad_wb = jnp.concatenate([total[0, : TAPS * 96], total[1, : TAPS * 96]], axis=1)
        first = total[0, STORED : STORED + 14 * 96, :96]
        second = total[1, STORED : STORED + 13 * 96, :96]
        grad_wa = jnp.concatenate([first, second], axis=0)
        layer_out = layer(1, zh, wbt, layer(0, zh, wbt))
        return layer_out, data_grad(zp), grad_wa.reshape(TAPS, 96, 96), grad_wb.reshape(TAPS, 96, 256)

    along_y = ("gx", [(k, k ^ 2) for k in range(4)])
    along_x = ("gy", [(0, 1), (1, 0)])
    bit_y = lax.axis_index("gx") >> 1
    bit_x = lax.axis_index("gy")
    swap = ("gx", [(k, k ^ 1) for k in range(4)])
    keep, send = sums
    got = lax.ppermute(send, *swap)
    zh, zp = second(from_one, from_two, from_y)
    got, zh, zp = lax.optimization_barrier((got, zh, zp))
    send_a = half_sum(keep[0], got[0], 1 - bit_y).astype(BF)
    send_b = half_sum(keep[1], got[1], 1 - bit_x).astype(BF)
    send_a, send_b, keep, got, zh = lax.optimization_barrier((send_a, send_b, keep, got, zh))
    got_a = lax.ppermute(send_a, *along_y)
    got_b = lax.ppermute(send_b, *along_x)
    keep_a = half_sum(keep[0], got[0], bit_y)
    keep_b = half_sum(keep[1], got[1], bit_x)
    layer_out = layer(0, zh, wbt)
    got_a, got_b, layer_out, keep_a, keep_b = lax.optimization_barrier(
        (got_a, got_b, layer_out, keep_a, keep_b)
    )
    send_a, keep_a = swap_or_keep(keep_a + got_a.astype(F32), bit_x)
    send_b, keep_b = swap_or_keep(keep_b + got_b.astype(F32), bit_y)
    zh, send_a, send_b = lax.optimization_barrier((zh, send_a, send_b))
    other_a = lax.ppermute(send_a, *along_x)
    other_b = lax.ppermute(send_b, *along_y)
    layer_out = layer(1, zh, wbt, layer_out)
    other_a, other_b, layer_out = lax.optimization_barrier((other_a, other_b, layer_out))
    part_a = (keep_a + other_a.astype(F32)).astype(BF)
    part_b = (keep_b + other_b.astype(F32)).astype(BF)
    zp, part_a, part_b = lax.optimization_barrier((zp, part_a, part_b))
    other_a = lax.ppermute(part_a, *along_x)
    other_b = lax.ppermute(part_b, *along_y)
    grad_features = data_grad(zp)
    other_a, other_b, grad_features = lax.optimization_barrier((other_a, other_b, grad_features))

    def joined(piece, other, bit):
        first = bit == 0
        return jnp.concatenate(
            [jnp.where(first, piece, other), jnp.where(first, other, piece)], axis=0
        )

    part_a, part_b = joined(part_a, other_a, bit_x), joined(part_b, other_b, bit_y)
    other_a = lax.ppermute(part_a, *along_y)
    other_b = lax.ppermute(part_b, *along_x)
    mine = jnp.stack([joined(part_a, other_a, bit_y), joined(part_b, other_b, bit_x)], axis=0)
    other = lax.ppermute(mine, *swap)
    grad_wa, grad_wb = call(
        unpack_kernel,
        [((TAPS, 96, 96), F32), ((TAPS, 96, 256), F32)],
        [mine, other],
        [((2, HALF, 128), BF), ((TAPS, 96, 96), F32), ((TAPS, 96, 256), F32)],
        moved=6 * MIB,
        far_outs=2,
        sems=4,
        limit=20 * MIB,
    )
    return layer_out, grad_features, grad_wa, grad_wb


def solution(mesh):
    in_specs = (
        P(("dp", "gx", "gy"), None, None),
        P(("dp", "gx", "gy"), None),
        P(("dp", "gx", "gy"), None),
        P(("dp", "gx"), "gy", None),
        P(),
        P(),
        P(("dp", "gx", "gy"), None, None),
    )
    out_specs = (
        P(("dp", "gx", "gy"), None, None),
        P(("dp", "gx", "gy"), None, None),
        P("dp", None, None),
        P("dp", None, None),
    )
    return jax.shard_map(body, mesh=mesh, in_specs=in_specs, out_specs=out_specs, check_vma=False)
```

```python
import functools

import jax
import jax.numpy as jnp
from jax import lax
from jax.experimental import pallas as pl
from jax.experimental.pallas import tpu as pltpu
from jax.sharding import PartitionSpec as P

EDGE = 8
VOX = 512
TAPS = 27
PLANE = 80
PADDED = 896
OUTER = 640
FIRST = 88
FACE = 128
FAR = 100
HALO = 512
HALF = 3712
STORED = 2592
USED = 3600
NT = (((1,), (1,)), ((), ()))
BF = jnp.bfloat16
F32 = jnp.float32
VMEM = pl.BlockSpec(memory_space=pltpu.VMEM)
FAR_SPEC = pl.BlockSpec(memory_space=pltpu.HBM)
SMEM = pl.BlockSpec(memory_space=pltpu.SMEM)
LIMIT = 58 * 1024 * 1024
MIB = 1024 * 1024


def iota(shape, dim):
    return lax.broadcasted_iota(jnp.int32, shape, dim)


def one_hot(cond):
    return jnp.where(cond, 1.0, 0.0).astype(BF)


def slot_places(send_ref):
    places = []
    for slot in range(2):
        px = py = pz = held = jnp.int32(0)
        for x in range(2):
            for y in range(2):
                for z in range(2):
                    here = (send_ref[x, y, z] == slot).astype(jnp.int32)
                    held = held + here
                    px = px + here * x
                    py = py + here * y
                    pz = pz + here * z
        places.append((px, py, pz, held))
    return places


def lane_mask(occ_ref, slot, width, plane):
    lane = iota((8, width), 1)
    if plane == 64:
        voxel = lane
        inside = lane >= 0
    else:
        x = lax.shift_right_logical(lane * 205, 14)
        rest = lane - x * plane
        voxel = x * 64 + rest
        inside = rest < 64
    word = lax.shift_right_logical(voxel * 2185, 16)
    bit = voxel - word * 30
    total = jnp.zeros((8, width), jnp.int32)
    for w in range(18):
        total = jnp.where(word == w, occ_ref[slot, w], total)
    on = lax.shift_right_logical(total, bit) & 1
    return jnp.where(inside, on, 0).astype(F32)[:1]


def y_side(dirs, q, receiving):
    if dirs == 1:
        return 1 - lax.axis_index("gy")
    return q if receiving else 1 - q


def x_side(which):
    odd = lax.axis_index("gx") & 1
    return odd if which else 1 - odd


def send_choices(send_ref, dirs):
    places = slot_places(send_ref)

    def split(row):
        return row >> 6, (row >> 3) & 7, row & 7

    along_x = []
    lane = iota((FACE, FACE), 1)
    for which in range(2):
        side = x_side(which)
        i, j, l = split(iota((FACE, FACE), 0) + 384 * side)
        ahead = jnp.int32(0)
        picks = []
        for px, py, pz, held in places:
            facing = (px == side).astype(jnp.int32) * held
            at_face = i == 7 * side
            blocks = [
                one_hot(jnp.where(at_face & (facing == 1), ahead * 64 + j * 8 + l, -1) == lane)
            ]
            ahead = ahead + facing
            for q in range(dirs):
                col = y_side(dirs, q, False)
                here = at_face & (j == 7 * col) & ((facing == 1) & (py == col))
                edge = jnp.where(here, 16 * (1 - side) + pz * 8 + l, -1)
                blocks.append(one_hot(edge == (lane & 31)))
            picks.append(jnp.concatenate(blocks, axis=1))
        along_x.append(picks)
    along_y = []
    lane = iota((VOX, FACE), 1)
    i, j, l = split(iota((VOX, FACE), 0))
    for q in range(dirs):
        col = y_side(dirs, q, False)
        ahead = jnp.int32(0)
        picks = []
        for px, py, pz, held in places:
            facing = (py == col).astype(jnp.int32) * held
            here = (j == 7 * col) & (facing == 1)
            picks.append(one_hot(jnp.where(here, ahead * 64 + i * 8 + l, -1) == lane))
            ahead = ahead + facing
        along_y.append(picks)
    return along_x, along_y


def pack_sends(own_ref, send_ref, dirs, one_ref, two_ref, y_ref):
    channels = own_ref.shape[1]
    group = channels // 4
    along_x, along_y = send_choices(send_ref, dirs)
    glane = iota((group, FACE), 1) >> 5
    for which, (picks, ref) in enumerate(zip(along_x, (one_ref, two_ref))):
        lanes = pl.ds(pl.multiple_of(384 * x_side(which), 128), 128)
        wide = jnp.dot(own_ref[0, :, lanes], picks[0], preferred_element_type=F32) + jnp.dot(
            own_ref[1, :, lanes], picks[1], preferred_element_type=F32
        )
        ref[:channels, :] = wide[:, :FACE].astype(BF)
        for q in range(dirs):
            at = FACE * (1 + q)
            packed = jnp.zeros((group, FACE), F32)
            for g in range(4):
                packed = jnp.where(
                    glane == g, wide[group * g : group * g + group, at : at + FACE], packed
                )
            ref[channels + group * q : channels + group * q + group, :] = packed.astype(BF)
    for q in range(dirs):
        y_ref[q, :, :] = (
            jnp.dot(own_ref[0], along_y[q][0], preferred_element_type=F32)
            + jnp.dot(own_ref[1], along_y[q][1], preferred_element_type=F32)
        ).astype(BF)


def ring_of(x, y):
    return jnp.where(x == 0, y, jnp.where(x == 9, 10 + y, jnp.where(y == 0, 19 + x, 27 + x)))


def encode(x, y, z, ok):
    ok = ok & (x >= 0) & (x <= 9) & (y >= 0) & (y <= 9) & (z >= -1) & (z <= 8)
    side = ring_of(x, y) * 8 + z
    ends = 288 + (x * 10 + y) * 2 + jnp.where(z > 7, 1, 0)
    return jnp.where(ok, jnp.where((z < 0) | (z > 7), ends, side), -1)


def halo_choice(so_ref, sr_ref, n, send_ref, near_ref, dirs):
    places = slot_places(send_ref)
    nx, ny, nz, _ = places[n]
    px, py, pz, _ = places[1 - n]

    def put(ref, at, rows, target):
        for b in range(HALO // 128):
            ref[n, at : at + rows, 128 * b : 128 * b + 128] = one_hot(
                target == iota((rows, 128), 1) + 128 * b
            )

    row = iota((VOX, 128), 0)
    put(
        so_ref,
        0,
        VOX,
        encode(
            (row >> 6) + 1 + 8 * (px - nx),
            ((row >> 3) & 7) + 1 + 8 * (py - ny),
            (row & 7) + 8 * (pz - nz),
            row >= 0,
        ),
    )

    def ranked(offset_of):
        count = jnp.int32(0)
        firsts = [jnp.int32(FAR), jnp.int32(FAR)]
        depths = [jnp.int32(0), jnp.int32(0)]
        for across in range(2):
            for z in range(2):
                there = (near_ref[n, offset_of(across, z)] >= 0).astype(jnp.int32)
                for rank in range(2):
                    take = (there == 1) & (count == rank)
                    firsts[rank] = jnp.where(take, across, firsts[rank])
                    depths[rank] = jnp.where(take, z, depths[rank])
                count = count + there
        return firsts, depths

    row = iota((FACE, 128), 0)
    high = row >= 64
    u = (row >> 3) & 7
    l = row & 7
    nought = jnp.zeros((FACE, 128), jnp.int32)
    firsts, depths = ranked(
        lambda across, z: 18 * nx + 3 * (across - ny + 1) + (z - nz + 1)
    )
    across = jnp.where(high, firsts[1], firsts[0])
    depth = jnp.where(high, depths[1], depths[0])
    for which in range(2):
        side = x_side(which)
        put(
            sr_ref,
            FACE * which,
            FACE,
            encode(
                nought + 9 * side,
                u + 1 + 8 * (across - ny),
                l + 8 * (depth - nz),
                nought + nx == side,
            ),
        )
    firsts, depths = ranked(
        lambda across, z: 9 * (across - nx + 1) + 6 * ny + (z - nz + 1)
    )
    across = jnp.where(high, firsts[1], firsts[0])
    depth = jnp.where(high, depths[1], depths[0])
    e = row & 31
    from_side = e >> 4
    for q in range(dirs):
        side = y_side(dirs, q, True)
        put(
            sr_ref,
            FACE * (2 + q),
            FACE,
            encode(
                u + 1 + 8 * (across - nx),
                nought + 9 * side,
                l + 8 * (depth - nz),
                nought + ny == side,
            ),
        )
        put(
            sr_ref,
            FACE * (2 + dirs + q),
            FACE,
            encode(
                9 * from_side,
                nought + 9 * side,
                (e & 7) + 8 * (((e >> 3) & 1) - nz),
                (from_side == nx) & (nought + ny == side),
            ),
        )


def padded_choice(stat_ref):
    lane = iota((8, PADDED), 1)
    x = lax.shift_right_logical(lane * 205, 14)
    rest = lane - x * PLANE
    y = rest >> 3
    l = rest & 7
    within = (x >= 1) & (x <= 8) & (y >= 1) & (y <= 8)
    own = jnp.where(within, (x - 1) * 64 + (y - 1) * 8 + l, -1)
    side = jnp.where(within | (x > 9), -1, ring_of(x, y) * 8 + l)
    ends = jnp.where(
        (x <= 9) & ((l == 0) | (l == 7)), 288 + (x * 10 + y) * 2 + jnp.where(l == 7, 1, 0), -1
    )
    row = iota((HALO, PADDED), 0)
    for index, target in enumerate((own, side, ends)):
        stat_ref[index] = one_hot(row == target[:1])


def fill_padded(own_ref, part_ref, recv_one, recv_two, recv_y, sr_ref, stat_ref, d_ref, xh_ref, dirs, outs):
    channels = own_ref.shape[1]
    group = channels // 4
    d_ref[:, :FACE] = recv_one[:channels, :]
    d_ref[:, FACE : 2 * FACE] = recv_two[:channels, :]
    glane = iota((group, FACE), 1) >> 5
    for q in range(dirs):
        at = FACE * (2 + q)
        d_ref[:, at : at + FACE] = recv_y[q, :channels, :]
        packed = recv_y[q, channels : channels + group, :].astype(F32)
        spread = jnp.concatenate([jnp.where(glane == g, packed, 0.0) for g in range(4)], axis=0)
        at = FACE * (2 + dirs + q)
        d_ref[:, at : at + FACE] = spread.astype(BF)
    halos = [jnp.dot(d_ref[...], sr_ref[n], preferred_element_type=F32) for n in range(2)]
    for n in range(2):
        rows = slice(channels * n, channels * n + channels)
        xh_ref[rows, :VOX] = own_ref[n]
        xh_ref[rows, VOX:] = (halos[n] + part_ref[n].astype(F32)).astype(BF)
    middle = jnp.dot(xh_ref[:, :VOX], stat_ref[0], preferred_element_type=F32) + jnp.dot(
        xh_ref[:, VOX:], stat_ref[1], preferred_element_type=F32
    )
    ends = jnp.dot(xh_ref[:, VOX:], stat_ref[2], preferred_element_type=F32)
    for ref, first, count, flip in outs:
        l = iota((count, PADDED), 1) & 7
        for n in range(2):
            rows = slice(channels * n + first, channels * n + first + count)
            mid = middle[rows]
            end = ends[rows]
            at = slice(PADDED * n, PADDED * n + PADDED)
            below = jnp.where(l == 0, end, pltpu.roll(mid, 1, 1)).astype(BF)
            above = jnp.where(l == 7, end, pltpu.roll(mid, PADDED - 1, 1)).astype(BF)
            low, high = (above, below) if flip else (below, above)
            ref[:count, at] = low
            ref[count : 2 * count, at] = mid.astype(BF)
            ref[2 * count :, at] = high


def shifted_sum(s_ref, n, flip):
    total = None
    for ab in range(9):
        a, b = ab // 3, ab % 3
        if flip:
            a, b = 2 - a, 2 - b
        at = PADDED * n + PLANE * a + 8 * b
        part = s_ref[96 * ab : 96 * ab + 96, at : at + OUTER]
        total = part if total is None else total + part
    return total


def compaction():
    row = iota((OUTER, VOX), 0)
    x = lax.shift_right_logical(row * 205, 14)
    rest = row - x * PLANE
    return one_hot(jnp.where(rest < 64, x * 64 + rest, -1) == iota((OUTER, VOX), 1))


def pack_kernel(dirs, feat_ref, cot_ref, occ_ref, send_ref, own_ref, one_ref, two_ref, y_ref):
    for n in range(2):
        mask = lane_mask(occ_ref, n, VOX, 64)
        own_ref[n, :96, :] = jnp.where(mask > 0.5, feat_ref[n].astype(F32), 0.0).astype(BF)
        own_ref[n, 96:, :] = jnp.where(mask > 0.5, cot_ref[n].astype(F32), 0.0).astype(BF)
    pack_sends(own_ref, send_ref, dirs, one_ref, two_ref, y_ref)


def halo_kernel(dirs, own_ref, near_ref, send_ref, so_ref, sr_ref, part_ref):
    for n in range(2):
        halo_choice(so_ref, sr_ref, n, send_ref, near_ref, dirs)
    for n in range(2):
        part_ref[n] = jnp.dot(own_ref[1 - n], so_ref[n], preferred_element_type=F32).astype(BF)


def layout_kernel(wa_ref, wb_ref, stat_ref, wa9_ref, wbt_ref):
    padded_choice(stat_ref)
    for k in range(TAPS):
        c, ab = k % 3, k // 3
        wa9_ref[96 * ab : 96 * ab + 96, 96 * c : 96 * c + 96] = wa_ref[k].astype(F32).T.astype(BF)
        wbt_ref[:, 96 * k : 96 * k + 96] = wb_ref[k].astype(F32).T.astype(BF)


def first_kernel(
    dirs, f1_ref, f2_ref, fy_ref, sr_ref, occ_ref, send_ref, own_ref, part_ref, stat_ref, wa_ref, wb_ref,
    zx_ref, zg_ref, gpre_ref, wide_ref, hid_ref, one_ref, two_ref, y_ref,
    d_ref, xh_ref, s9_ref, pre_ref, wb9_ref,
):
    fill_padded(
        own_ref, part_ref, f1_ref, f2_ref, fy_ref, sr_ref, stat_ref, d_ref, xh_ref, dirs,
        ((zx_ref, 0, 96, False), (zg_ref, 96, 256, True)),
    )
    s9_ref[...] = jnp.dot(wa_ref[...], zx_ref[...], preferred_element_type=F32)
    for n in range(2):
        pre_ref[:, OUTER * n : OUTER * n + OUTER] = shifted_sum(s9_ref, n, False)
    for k in range(TAPS):
        c, ab = k % 3, k // 3
        wb9_ref[96 * ab : 96 * ab + 96, 256 * c : 256 * c + 256] = wb_ref[k]
    s9_ref[...] = jnp.dot(wb9_ref[...], zg_ref[...], preferred_element_type=F32)
    squeeze = compaction()
    for n in range(2):
        at = slice(OUTER * n, OUTER * n + OUTER)
        mask = lane_mask(occ_ref, n, OUTER, PLANE)
        pre = pre_ref[:, at] * mask
        gate = 1.0 / (1.0 + jnp.exp(-pre))
        hidden = (pre * gate).astype(BF)
        grad_pre = (
            shifted_sum(s9_ref, n, True) * gate * (1.0 + pre * (1.0 - gate)) * mask
        ).astype(BF)
        gpre_ref[:, at] = grad_pre
        wide_ref[:, at] = hidden
        both = jnp.concatenate([hidden, grad_pre], axis=0)
        hid_ref[n] = jnp.dot(both, squeeze, preferred_element_type=F32).astype(BF)
    pack_sends(hid_ref, send_ref, dirs, one_ref, two_ref, y_ref)


def tile_rows(tile):
    if tile < 3:
        return [(0, STORED + 288 * tile, 0, 288)]
    if tile > 3:
        return [(1, STORED + 288 * (tile - 4), 0, 288)]
    return [(0, STORED + 864, 0, 144), (1, STORED + 864, 144, 144)]


def weights_kernel(scale, split, zx_ref, zg_ref, gpre_ref, wide_ref, keep_ref, *rest):
    g9_ref, h9_ref, sum_ref = rest[-3:]
    h9_ref[...] = jnp.zeros_like(h9_ref)
    g9_ref[...] = jnp.zeros_like(g9_ref)
    for ab in range(9):
        for n in range(2):
            own = slice(OUTER * n, OUTER * n + OUTER)
            at = PADDED * n + PLANE * (2 - ab // 3) + 8 * (2 - ab % 3)
            h9_ref[96 * ab : 96 * ab + 96, at : at + OUTER] = wide_ref[:, own]
            at = PADDED * n + PLANE * (ab // 3) + 8 * (ab % 3)
            g9_ref[96 * ab : 96 * ab + 96, at : at + OUTER] = gpre_ref[:, own]
    total = scale * lax.dot_general(h9_ref[...], zg_ref[...], NT, preferred_element_type=F32)
    sum_ref[:, USED:, :] = jnp.zeros((2, HALF - USED, 128), F32)
    for k in range(TAPS):
        c, ab = k % 3, k // 3
        for half in range(2):
            sum_ref[half, 96 * k : 96 * k + 96, :] = total[
                96 * ab : 96 * ab + 96, 256 * c + 128 * half : 256 * c + 128 * half + 128
            ]
    total = scale * lax.dot_general(zx_ref[...], g9_ref[...], NT, preferred_element_type=F32)
    for tile in range(7):
        for half, at, start, rows in tile_rows(tile):
            sum_ref[half, at : at + rows, :] = total[start : start + rows, 128 * tile : 128 * tile + 128]
    if split:
        core = lax.axis_index("gx") & 1
        keep = pl.multiple_of(core * (HALF // 2), HALF // 2)
        send = pl.multiple_of((1 - core) * (HALF // 2), HALF // 2)
        keep_ref[...] = sum_ref[:, pl.ds(keep, HALF // 2), :]
        rest[0][...] = sum_ref[:, pl.ds(send, HALF // 2), :].astype(BF)
    else:
        keep_ref[...] = sum_ref[...]


def second_kernel(
    dirs, f1_ref, f2_ref, fy_ref, sr_ref, so_ref, own_ref, stat_ref, zh_ref, zp_ref, d_ref, xh_ref, part_ref
):
    for n in range(2):
        part_ref[n] = jnp.dot(own_ref[1 - n], so_ref[n], preferred_element_type=F32).astype(BF)
    fill_padded(
        own_ref, part_ref, f1_ref, f2_ref, fy_ref, sr_ref, stat_ref, d_ref, xh_ref, dirs,
        ((zh_ref, 0, 96, False), (zp_ref, 96, 96, True)),
    )


def out_kernel(n, occ_ref, zh_ref, wbt_ref, *rest):
    out_hbm, p_ref, out_ref, sem = rest[-4:]
    for k in range(TAPS):
        a, b, c = k // 9, k // 3 % 3, k % 3
        at = PADDED * n + PLANE * a + 8 * b
        p_ref[96 * k : 96 * k + 96, :] = zh_ref[96 * c : 96 * c + 96, at : at + OUTER]
    total = jnp.dot(wbt_ref[...], p_ref[...], preferred_element_type=F32)
    total = (total * lane_mask(occ_ref, n, OUTER, PLANE)).astype(BF)
    out_ref[...] = jnp.dot(total, compaction(), preferred_element_type=F32).astype(BF)
    store = pltpu.make_async_copy(out_ref, out_hbm.at[n], sem.at[0])
    store.start()
    store.wait()


def grad_kernel(occ_ref, zp_ref, wa_ref, grad_ref, s9_ref, wg9_ref):
    for k in range(TAPS):
        c, ab = k % 3, k // 3
        wg9_ref[96 * ab : 96 * ab + 96, 96 * c : 96 * c + 96] = wa_ref[k]
    s9_ref[...] = jnp.dot(wg9_ref[...], zp_ref[...], preferred_element_type=F32)
    squeeze = compaction()
    for n in range(2):
        mask = lane_mask(occ_ref, n, OUTER, PLANE)
        grad_ref[n] = jnp.dot(
            (shifted_sum(s9_ref, n, True) * mask).astype(BF), squeeze, preferred_element_type=F32
        ).astype(BF)


def unpack_kernel(mine_ref, other_ref, wa_hbm, wb_hbm, all_ref, wa_ref, wb_ref, sems):
    core = lax.axis_index("gx") & 1
    for index, ref in enumerate((mine_ref, other_ref)):
        at = core if index == 0 else 1 - core
        at = pl.multiple_of(at * (HALF // 2), HALF // 2)
        all_ref[:, pl.ds(at, HALF // 2), :] = ref[...]
    copies = []

    def store(source, target):
        copies.append(pltpu.make_async_copy(source, target, sems.at[len(copies)]))
        copies[-1].start()

    for k in range(TAPS):
        for side in range(2):
            wb_ref[k, :, 128 * side : 128 * side + 128] = all_ref[
                side, 96 * k : 96 * k + 96, :
            ].astype(F32)
        if k % 9 == 8:
            store(wb_ref.at[pl.ds(k - 8, 9)], wb_hbm.at[pl.ds(k - 8, 9)])
    tiles = []
    for tile in range(7):
        parts = [all_ref[half, at : at + rows, :].astype(F32) for half, at, _, rows in tile_rows(tile)]
        tiles.append(parts[0] if len(parts) == 1 else jnp.concatenate(parts, axis=0))
    total = jnp.concatenate(tiles, axis=1)
    for k in range(TAPS):
        c, ab = k % 3, k // 3
        wa_ref[k] = total[96 * c : 96 * c + 96, 96 * ab : 96 * ab + 96]
    store(wa_ref, wa_hbm)
    for copy in copies:
        copy.wait()


def call(kernel, outs, ins, scratch=(), flops=0, moved=0, far_ins=0, far_outs=0, sems=0, limit=LIMIT, aliases={}):
    specs = [SMEM if jnp.issubdtype(x.dtype, jnp.integer) else VMEM for x in ins]
    for k in range(far_ins):
        specs[len(ins) - 1 - k] = FAR_SPEC
    out_specs = [VMEM] * len(outs)
    for k in range(far_outs):
        out_specs[k] = FAR_SPEC
    scratch = [pltpu.VMEM(s, d) for s, d in scratch]
    if sems:
        scratch.append(pltpu.SemaphoreType.DMA((sems,)))
    return pl.pallas_call(
        kernel,
        out_shape=[jax.ShapeDtypeStruct(s, d) for s, d in outs],
        in_specs=specs,
        out_specs=out_specs,
        scratch_shapes=scratch,
        input_output_aliases=aliases,
        compiler_params=pltpu.CompilerParams(vmem_limit_bytes=limit),
        cost_estimate=pl.CostEstimate(flops=flops, bytes_accessed=moved, transcendentals=0),
    )(*ins)


def exchange_x(one, two, count_x):
    def pairs(first):
        starts = range(first, count_x - 1, 2)
        return [(k, k + 1) for k in starts] + [(k + 1, k) for k in starts]

    return lax.ppermute(one, "gx", pairs(0)), lax.ppermute(two, "gx", pairs(1))


def exchange_y(channels, faces, from_one, from_two, count_y):
    group = channels // 4
    dirs = faces.shape[0]
    if dirs == 1:
        perms = [[(0, 1), (1, 0)]]
    else:
        perms = [
            [(k, k + 1) for k in range(count_y - 1)],
            [(k + 1, k) for k in range(count_y - 1)],
        ]
    arrived = []
    for q in range(dirs):
        at = channels + group * q
        edges = from_one[at : at + group] + from_two[at : at + group]
        arrived.append(
            lax.ppermute(jnp.concatenate([faces[q], edges], axis=0), "gy", perms[q])
        )
    return jnp.stack(arrived, axis=0)


def half_rows(piece, which):
    rows = piece.shape[0] // 2
    return lax.dynamic_slice_in_dim(piece, which * rows, rows, axis=0)


def swap_or_keep(piece, bit):
    rows = piece.shape[0] // 2
    low, high = piece[:rows], piece[rows:]
    return jnp.where(bit == 0, high, low).astype(BF), jnp.where(bit == 0, low, high)


def half_sum(kept, got, which):
    return half_rows(kept, which) + half_rows(got, which).astype(F32)


def body(features, occupancy, neighbours, send_slots, weight_a, weight_b, cotangent):
    count_x = lax.axis_size("gx")
    count_y = lax.axis_size("gy")
    dirs = 1 if count_y == 2 else 2
    split = count_x == 4 and count_y == 2
    scale = float(features.shape[0] * VOX * count_x * count_y) ** -0.5
    lanes = FACE * (2 + 2 * dirs)
    wide = 2 * PADDED
    outer = 2 * OUTER

    rows = 352 + 88 * dirs
    own, one, two, faces = call(
        functools.partial(pack_kernel, dirs),
        [((2, 352, VOX), BF), ((rows, FACE), BF), ((rows, FACE), BF), ((dirs, 352, FACE), BF)],
        [features, cotangent, occupancy, send_slots],
        flops=352 * 1024 * 1024,
        moved=2 * 1024 * 1024,
    )

    from_one, from_two = exchange_x(one, two, count_x)
    halo_own, halo_far, part = call(
        functools.partial(halo_kernel, dirs),
        [((2, VOX, HALO), BF), ((2, lanes, HALO), BF), ((2, 352, HALO), BF)],
        [own, neighbours, send_slots],
        flops=10**9,
        moved=4 * MIB,
    )
    faces, part = lax.optimization_barrier((faces, part))
    from_y = exchange_y(352, faces, from_one, from_two, count_y)
    weight_a, weight_b, part = lax.optimization_barrier((weight_a, weight_b, part))
    padded, wa9, wbt = call(
        layout_kernel,
        [((3, HALO, PADDED), BF), ((864, 288), BF), ((256, TAPS * 96), BF)],
        [weight_a, weight_b],
        moved=6 * MIB,
        flops=10**8,
        limit=8 * MIB,
    )
    from_y, padded = lax.optimization_barrier((from_y, padded))

    rows = 192 + 48 * dirs
    zx, zg, gpre, hidden, hid, one, two, faces = call(
        functools.partial(first_kernel, dirs),
        [
            ((288, wide), BF),
            ((768, wide), BF),
            ((96, outer), BF),
            ((96, outer), BF),
            ((2, 192, VOX), BF),
            ((rows, FACE), BF),
            ((rows, FACE), BF),
            ((dirs, 192, FACE), BF),
        ],
        [
            from_one, from_two, from_y, halo_far, occupancy, send_slots,
            own, part, padded, wa9, weight_b,
        ],
        [
            ((352, lanes), BF),
            ((704, 1024), BF),
            ((864, wide), F32),
            ((96, outer), F32),
            ((864, 768), BF),
        ],
        flops=5 * 10**9,
        moved=8 * MIB,
        limit=20 * MIB,
    )
    from_one, from_two = exchange_x(one, two, count_x)
    sums = [((2, HALF, 128), F32)]
    if split:
        sums = [((2, HALF // 2, 128), F32), ((2, HALF // 2, 128), BF)]
    sums = call(
        functools.partial(weights_kernel, scale, split),
        sums,
        [zx, zg, gpre, hidden],
        [((7 * 128, wide), BF), ((9 * 96, wide), BF), ((2, HALF, 128), F32)],
        flops=5 * 10**9,
        moved=6 * MIB,
        limit=24 * MIB,
    )

    from_one, from_two, sums = lax.optimization_barrier((from_one, from_two, sums))
    from_y = exchange_y(192, faces, from_one, from_two, count_y)

    def second(from_one, from_two, from_y):
        return call(
            functools.partial(second_kernel, dirs),
            [((288, wide), BF), ((288, wide), BF)],
            [from_one, from_two, from_y, halo_far, halo_own, hid, padded],
            [((192, lanes), BF), ((384, 1024), BF), ((2, 192, HALO), BF)],
            flops=2 * 10**9,
            moved=6 * MIB,
            limit=14 * MIB,
        )

    def layer(n, zh, wbt, *earlier):
        return call(
            functools.partial(out_kernel, n),
            [((2, 256, VOX), BF)],
            [occupancy, zh, wbt, *earlier],
            [((TAPS * 96, OUTER), BF), ((256, VOX), BF)],
            flops=10**9,
            moved=2 * MIB,
            far_ins=len(earlier),
            far_outs=1,
            sems=1,
            limit=12 * MIB,
            aliases={3: 0} if earlier else {},
        )[0]

    def data_grad(zp):
        return call(
            grad_kernel,
            [((2, 96, VOX), BF)],
            [occupancy, zp, weight_a],
            [((864, wide), F32), ((864, 288), BF)],
            flops=2 * 10**9,
            moved=2 * MIB,
            limit=14 * MIB,
        )[0]

    if not split:
        zh, zp = second(from_one, from_two, from_y)
        total = lax.psum(sums[0], ("gx", "gy"))
        grad_wb = jnp.concatenate([total[0, : TAPS * 96], total[1, : TAPS * 96]], axis=1)
        tiles = []
        for tile in range(7):
            parts = [total[half, at : at + rows] for half, at, _, rows in tile_rows(tile)]
            tiles.append(jnp.concatenate(parts, axis=0))
        grad_wa = jnp.concatenate(tiles, axis=1)[:, :864].reshape(3, 96, 9, 96)
        grad_wa = grad_wa.transpose(2, 0, 1, 3)
        layer_out = layer(1, zh, wbt, layer(0, zh, wbt))
        return layer_out, data_grad(zp), grad_wa.reshape(TAPS, 96, 96), grad_wb.reshape(TAPS, 96, 256)

    along_y = ("gx", [(k, k ^ 2) for k in range(4)])
    along_x = ("gy", [(0, 1), (1, 0)])
    bit_y = lax.axis_index("gx") >> 1
    bit_x = lax.axis_index("gy")
    swap = ("gx", [(k, k ^ 1) for k in range(4)])
    keep, send = sums
    got = lax.ppermute(send, *swap)
    zh, zp = second(from_one, from_two, from_y)
    got, zh, zp = lax.optimization_barrier((got, zh, zp))
    send_a = half_sum(keep[0], got[0], 1 - bit_y).astype(BF)
    send_b = half_sum(keep[1], got[1], 1 - bit_x).astype(BF)
    send_a, send_b, keep, got, zh = lax.optimization_barrier((send_a, send_b, keep, got, zh))
    got_a = lax.ppermute(send_a, *along_y)
    got_b = lax.ppermute(send_b, *along_x)
    keep_a = half_sum(keep[0], got[0], bit_y)
    keep_b = half_sum(keep[1], got[1], bit_x)
    layer_out = layer(0, zh, wbt)
    got_a, got_b, layer_out, keep_a, keep_b = lax.optimization_barrier(
        (got_a, got_b, layer_out, keep_a, keep_b)
    )
    send_a, keep_a = swap_or_keep(keep_a + got_a.astype(F32), bit_x)
    send_b, keep_b = swap_or_keep(keep_b + got_b.astype(F32), bit_y)
    zh, send_a, send_b = lax.optimization_barrier((zh, send_a, send_b))
    other_a = lax.ppermute(send_a, *along_x)
    other_b = lax.ppermute(send_b, *along_y)
    layer_out = layer(1, zh, wbt, layer_out)
    other_a, other_b, layer_out = lax.optimization_barrier((other_a, other_b, layer_out))
    part_a = (keep_a + other_a.astype(F32)).astype(BF)
    part_b = (keep_b + other_b.astype(F32)).astype(BF)
    zp, part_a, part_b = lax.optimization_barrier((zp, part_a, part_b))
    other_a = lax.ppermute(part_a, *along_x)
    other_b = lax.ppermute(part_b, *along_y)
    grad_features = data_grad(zp)
    other_a, other_b, grad_features = lax.optimization_barrier((other_a, other_b, grad_features))

    def joined(piece, other, bit):
        first = bit == 0
        return jnp.concatenate(
            [jnp.where(first, piece, other), jnp.where(first, other, piece)], axis=0
        )

    part_a, part_b = joined(part_a, other_a, bit_x), joined(part_b, other_b, bit_y)
    other_a = lax.ppermute(part_a, *along_y)
    other_b = lax.ppermute(part_b, *along_x)
    mine = jnp.stack([joined(part_a, other_a, bit_y), joined(part_b, other_b, bit_x)], axis=0)
    other = lax.ppermute(mine, *swap)
    grad_wa, grad_wb = call(
        unpack_kernel,
        [((TAPS, 96, 96), F32), ((TAPS, 96, 256), F32)],
        [mine, other],
        [((2, HALF, 128), BF), ((TAPS, 96, 96), F32), ((TAPS, 96, 256), F32)],
        moved=6 * MIB,
        far_outs=2,
        sems=4,
        limit=20 * MIB,
    )
    return layer_out, grad_features, grad_wa, grad_wb


def solution(mesh):
    in_specs = (
        P(("dp", "gx", "gy"), None, None),
        P(("dp", "gx", "gy"), None),
        P(("dp", "gx", "gy"), None),
        P(("dp", "gx"), "gy", None),
        P(),
        P(),
        P(("dp", "gx", "gy"), None, None),
    )
    out_specs = (
        P(("dp", "gx", "gy"), None, None),
        P(("dp", "gx", "gy"), None, None),
        P("dp", None, None),
        P("dp", None, None),
    )
    return jax.shard_map(body, mesh=mesh, in_specs=in_specs, out_specs=out_specs, check_vma=False)
```
